32 devices in a mesh: grp: 2 (over x), row: 8 (over z, y), col: 2 (over core).
Axes of the slice: x: 2, y: 2, z: 4, core: 2. Of those that a mesh axis runs over, the one named last changes fastest.
Arguments:
- order_field: float32 [4, 16, 1024, 1024], P('grp', None, 'row', 'col'), may hold values from 0 to 1
- grain_label: int32 [4, 1024, 1024], P('grp', 'row', 'col'), may hold values from 0 to 31
- phase_label: int32 [4, 1024, 1024], P('grp', 'row', 'col'), may hold values from 0 to 7
- grain_mobility: float32 [32], replicated, may hold values from 0.25 to 1
- stiff_index: int32 [8], replicated, may hold values from 0 to 3
- stiff_table: float32 [4, 2], replicated, may hold values from 0.5 to 2
- eigen_strain: float32 [16, 3], replicated, may hold values from -1.5 to 1.5
- macro_strain: float32 [3], replicated, may hold values from -2 to 2
Outputs:
- order_next: float32 [4, 16, 1024, 1024], P('grp', None, 'row', 'col')
- strain_field: float32 [4, 3, 1024, 1024], P('grp', None, 'row', 'col')
The draws below stay inside these ranges and needn't reach their ends.
All inputs are finite; a program needn't handle non-finite values.
Results may differ from the reference program's by a relative error of at most 0.00014.
Values sent between devices are 32-bit elements; how exact they have to be, the bound alone decides.
No kernel may reach another device: no remote copies, remote signals or barrier semaphores. Data moves between devices by JAX's collectives and lax.ppermute only.
A program may use at most 192 MiB of HBM per device.

```python
import math
import jax
import jax.numpy as jnp
from jax import lax

NX = 1024
NY = 1024
NP = 16
ITERS = 2
GRAINS = 32
PHASES = 8
SETS = 4
LAYERS = 4


def draw_order_field(key, part):
    jitter_key = jax.random.fold_in(jax.random.fold_in(key, 11), 0)
    jitter = jax.random.uniform(jitter_key, (LAYERS, NP, NX, NY), jnp.float32)
    return jitter


def plant(values, key, smallest, largest):
    index_at = [jax.random.randint(jax.random.fold_in(key, axis), (), 0, length) for axis, length in enumerate(values.shape)]
    longest = values.shape.index(max(values.shape))
    next_to = index_at[:longest] + [(index_at[longest] + 1) % values.shape[longest]] + index_at[longest + 1:]
    return values.at[tuple(index_at)].set(smallest).at[tuple(next_to)].set(largest)


def gaussian(key, dims, width, limit, kind=jnp.bfloat16):
    values = jax.random.normal(key, dims, jnp.float32) * width
    return jnp.minimum(jnp.maximum(values, -limit), limit).astype(kind)


def setup_inputs(seed: int = 0) -> dict:
    streams_of = jax.random.split(jax.random.key(seed), 9)
    return {
        "order_field": draw_order_field(jax.random.fold_in(streams_of[8], 71), 0),
        "grain_label": plant(jax.random.randint(streams_of[1], (LAYERS, NX, NY), 0, GRAINS), jax.random.fold_in(streams_of[1], 1), 0, GRAINS - 1).astype(jnp.int32),
        "phase_label": plant(jax.random.randint(streams_of[2], (LAYERS, NX, NY), 0, PHASES), jax.random.fold_in(streams_of[2], 1), 0, PHASES - 1).astype(jnp.int32),
        "grain_mobility": jnp.clip(jnp.exp(jax.random.uniform(streams_of[3], (GRAINS,), jnp.float32, math.log(0.25), math.log(1.0))), 0.25, 1.0),
        "stiff_index": plant(jax.random.randint(streams_of[4], (PHASES,), 0, SETS), jax.random.fold_in(streams_of[4], 1), 0, SETS - 1).astype(jnp.int32),
        "stiff_table": jnp.clip(jnp.exp(jax.random.uniform(streams_of[5], (SETS, 2), jnp.float32, math.log(0.5), math.log(2.0))), 0.5, 2.0),
        "eigen_strain": gaussian(streams_of[6], (NP, 3), 0.3, 1.5, jnp.float32),
        "macro_strain": gaussian(streams_of[7], (3,), 0.5, 2.0, jnp.float32),
    }


GAMMA_MIX = 1.5
KAPPA_GRAD = 1.0
STEP_TIME = 0.1
LAYER_COUPLE = 0.5
LAMBDA_REF = 1.25
SHEAR_REF = 1.25
BETA_REF = (LAMBDA_REF + SHEAR_REF) / (SHEAR_REF * (LAMBDA_REF + 2.0 * SHEAR_REF))
PRECISE = lax.Precision.HIGHEST

def advance(fields, mobility, pad_fields, pad_mobility, below, above, driving_term):
    extent_rows = fields.shape[2]
    extent_cols = fields.shape[3]
    diffuse = jnp.zeros_like(fields)
    for offset_rows, offset_cols in ((0, 1), (2, 1), (1, 0), (1, 2)):
        beside = pad_fields[:, :, offset_rows:offset_rows + extent_rows, offset_cols:offset_cols + extent_cols]
        mob_beside = pad_mobility[:, None, offset_rows:offset_rows + extent_rows, offset_cols:offset_cols + extent_cols]
        diffuse = diffuse + 0.5 * (mobility[:, None] + mob_beside) * (beside - fields)
    squares = fields * fields
    totals = lax.optimization_barrier(jnp.sum(squares, axis=1, keepdims=True))
    bulk_term = squares * fields - fields + 2.0 * GAMMA_MIX * fields * (totals - squares)
    layered = LAYER_COUPLE * (below + above - 2.0 * fields)
    return fields + STEP_TIME * (KAPPA_GRAD * diffuse + mobility[:, None] * (layered - bulk_term + driving_term))

def directions(freq_rows, freq_cols, extent_rows, extent_cols):
    signed_rows = jnp.where(freq_rows >= extent_rows // 2, freq_rows - extent_rows, freq_rows).astype(jnp.float32)
    signed_cols = jnp.where(freq_cols >= extent_cols // 2, freq_cols - extent_cols, freq_cols).astype(jnp.float32)
    keeper = ((freq_rows != extent_rows // 2) & (freq_cols != extent_cols // 2)).astype(jnp.float32)
    radius = signed_rows * signed_rows + signed_cols * signed_cols
    inverse = keeper * lax.rsqrt(jnp.where(radius > 0, radius, 1.0))
    return (signed_rows * inverse, signed_cols * inverse)

def green(stress_rr, stress_cc, stress_rc, unit_row, unit_col):
    push_row = stress_rr * unit_row + stress_rc * unit_col
    push_col = stress_rc * unit_row + stress_cc * unit_col
    normal_part = unit_row * push_row + unit_col * push_col
    out_rr = unit_row * push_row / SHEAR_REF - BETA_REF * unit_row * unit_row * normal_part
    out_cc = unit_col * push_col / SHEAR_REF - BETA_REF * unit_col * unit_col * normal_part
    out_rc = 0.5 * (unit_row * push_col + unit_col * push_row) / SHEAR_REF - BETA_REF * unit_row * unit_col * normal_part
    return (out_rr, out_cc, out_rc)

def stress_of(strain, eigen_field, lambda_cell, shear_cell):
    elastic = strain - eigen_field
    along_rr = (lambda_cell + 2.0 * shear_cell) * elastic[:, 0] + lambda_cell * elastic[:, 1]
    along_cc = lambda_cell * elastic[:, 0] + (lambda_cell + 2.0 * shear_cell) * elastic[:, 1]
    along_rc = 2.0 * shear_cell * elastic[:, 2]
    return jnp.stack([along_rr, along_cc, along_rc], axis=1)

def driving(stress, fields, eigen_strain):
    weighted = jnp.stack([stress[:, 0], stress[:, 1], 2.0 * stress[:, 2]], axis=1)
    project = jnp.einsum('lcxy,ic->lixy', weighted, eigen_strain, precision=PRECISE)
    return 2.0 * fields * project

def reference(order_field, grain_label, phase_label, grain_mobility, stiff_index, stiff_table, eigen_strain, macro_strain):
    mobility = grain_mobility[grain_label]
    chosen = stiff_index[phase_label]
    lambda_cell = stiff_table[chosen, 0]
    shear_cell = stiff_table[chosen, 1]

    def step_fields(fields, driving_term):
        pad_fields = jnp.pad(fields, ((0, 0), (0, 0), (1, 1), (1, 1)), mode='wrap')
        pad_mobility = jnp.pad(mobility, ((0, 0), (1, 1), (1, 1)), mode='wrap')
        stacked = jnp.pad(fields, ((1, 1), (0, 0), (0, 0), (0, 0)))
        return advance(fields, mobility, pad_fields, pad_mobility, stacked[:-2], stacked[2:], driving_term)
    middle = step_fields(order_field, 0.0)
    eigen_field = jnp.einsum('lixy,ic->lcxy', middle * middle, eigen_strain, precision=PRECISE)
    freq_rows = jnp.arange(NX, dtype=jnp.int32)[:, None]
    freq_cols = jnp.arange(NY, dtype=jnp.int32)[None, :]
    unit_row, unit_col = directions(freq_rows, freq_cols, NX, NY)
    strain = jnp.broadcast_to(macro_strain[None, :, None, None], eigen_field.shape)
    for sweep_index in range(ITERS):
        stress = stress_of(strain, eigen_field, lambda_cell, shear_cell)
        spectrum = jnp.fft.fft2(stress)
        corrected = green(spectrum[:, 0], spectrum[:, 1], spectrum[:, 2], unit_row, unit_col)
        strain = strain - jnp.real(jnp.fft.ifft2(jnp.stack(corrected, axis=1)))
    stress = stress_of(strain, eigen_field, lambda_cell, shear_cell)
    updated = step_fields(middle, driving(stress, middle, eigen_strain))
    return (updated, strain)
```

```python
import math

import jax
import jax.numpy as jnp
import numpy as np
from jax import lax
from jax.experimental import pallas as pl
from jax.experimental.pallas import tpu as pltpu
from jax.sharding import PartitionSpec as P

ITERS = 2
GAMMA_MIX = 1.5
KAPPA_GRAD = 1.0
STEP_TIME = 0.1
LAYER_COUPLE = 0.5
LAMBDA_REF = 1.25
SHEAR_REF = 1.25
BETA_REF = (LAMBDA_REF + SHEAR_REF) / (SHEAR_REF * (LAMBDA_REF + 2.0 * SHEAR_REF))
STRIP = 8
RADIX = 4
VMEM_LIMIT = 56 * 1024 * 1024


def split3(value):
    high = value.astype(jnp.bfloat16)
    low = (value - high.astype(jnp.float32)).astype(jnp.bfloat16)
    return high, low


def dot3(left, right, dims):
    left_high, left_low = left
    right_high, right_low = right

    def product(a, b):
        return lax.dot_general(a, b, (dims, ((), ())), preferred_element_type=jnp.float32)

    return product(left_high, right_high) + (
        product(left_high, right_low) + product(left_low, right_high)
    )


def shift_rows(value, before, after):
    place = lax.broadcasted_iota(jnp.int32, value.shape, 0)
    size = value.shape[0]
    upper = jnp.where(place == 0, before, pltpu.roll(value, 1, 0))
    lower = jnp.where(place == size - 1, after, pltpu.roll(value, size - 1, 0))
    return upper, lower


def shift_cols(value, before, after):
    place = lax.broadcasted_iota(jnp.int32, value.shape, 1)
    size = value.shape[1]
    left = jnp.where(place == 0, before, pltpu.roll(value, 1, 1))
    right = jnp.where(place == size - 1, after, pltpu.roll(value, size - 1, 1))
    return left, right


def update_kernel(has_remote, final, count, *refs):
    refs = list(refs)
    refs.pop(0)
    phi, phi_up, phi_dn, other = (refs.pop(0) for _ in range(4))
    remote = refs.pop(0) if has_remote else None
    mob, mob_up, mob_dn = (refs.pop(0) for _ in range(3))
    edge_up, edge_dn, edge_col = (refs.pop(0) for _ in range(3))
    mob_edge_up, mob_edge_dn, mob_edge_col = (refs.pop(0) for _ in range(3))
    eigen_strain = refs.pop(0)
    if final:
        signs, macro, stiff, eigen = (refs.pop(0) for _ in range(4))
        swaps = [(refs.pop(0), refs.pop(0)) for _ in range(ITERS)]
        if has_remote:
            refs.pop(0)
            refs.pop(0)
        out, out_strain = refs
    else:
        out, out_eigen = refs
    block = pl.program_id(0)
    first = block == 0
    last = block == pl.num_programs(0) - 1
    rows = phi.shape[2]
    side = edge_col.shape[2] // 2
    mob_side = mob_edge_col.shape[2] // 2
    for start in range(0, rows, STRIP):
        stop = start + STRIP
        m = mob[0, start:stop, :]

        def before_after(main, up, dn, edge_before, edge_after):
            if start == 0:
                before = jnp.where(first, edge_before(), up(STRIP - 1))
            else:
                before = main(start - 1)
            if stop == rows:
                after = jnp.where(last, edge_after(), dn(0))
            else:
                after = main(stop)
            return before, after

        before, after = before_after(
            lambda r: mob[0, r : r + 1, :],
            lambda r: mob_up[0, r : r + 1, :],
            lambda r: mob_dn[0, r : r + 1, :],
            lambda: mob_edge_up[0, count : count + 1, :],
            lambda: mob_edge_dn[0, count : count + 1, :],
        )
        m_up, m_dn = shift_rows(m, before, after)
        m_edges = mob_edge_col[0, start:stop, :]
        m_left, m_right = shift_cols(
            m,
            m_edges[:, mob_side + count : mob_side + count + 1],
            m_edges[:, count : count + 1],
        )
        half_step = 0.5 * STEP_TIME * KAPPA_GRAD
        w_up = half_step * (m + m_up)
        w_dn = half_step * (m + m_dn)
        w_left = half_step * (m + m_left)
        w_right = half_step * (m + m_right)
        total = jnp.zeros_like(m)
        for i in range(count):
            value = phi[0, i, start:stop, :]
            total = total + value * value
        scaled = STEP_TIME * m
        base = (
            1.0
            - (w_up + w_dn + w_left + w_right)
            + scaled * ((1.0 - 2.0 * LAYER_COUPLE) - 2.0 * GAMMA_MIX * total)
        )
        coupling = LAYER_COUPLE * scaled
        cubic = (2.0 * GAMMA_MIX - 1.0) * scaled
        if final:
            sign = signs[0]
            lam = stiff[0, 0, start:stop, :]
            shear2 = 2.0 * stiff[0, 1, start:stop, :]
            elastic = []
            for c in range(3):
                strain = macro[c]
                for mine, theirs in swaps:
                    strain = strain - (
                        theirs[c, start:stop, :] + sign * mine[c, start:stop, :]
                    )
                out_strain[0, c, start:stop, :] = strain
                elastic.append(strain - eigen[c, start:stop, :])
            spread = lam * (elastic[0] + elastic[1])
            push = 2.0 * scaled
            sigma = (
                push * (spread + shear2 * elastic[0]),
                push * (spread + shear2 * elastic[1]),
                push * (2.0 * shear2 * elastic[2]),
            )
        else:
            sums = [jnp.zeros_like(m) for _ in range(3)]
        edges = edge_col[0, start:stop, :]
        for i in range(count):
            value = phi[0, i, start:stop, :]
            before, after = before_after(
                lambda r: phi[0, i, r : r + 1, :],
                lambda r: phi_up[0, i, r : r + 1, :],
                lambda r: phi_dn[0, i, r : r + 1, :],
                lambda: edge_up[0, i : i + 1, :],
                lambda: edge_dn[0, i : i + 1, :],
            )
            upper, lower = shift_rows(value, before, after)
            left, right = shift_cols(
                value, edges[:, side + i : side + i + 1], edges[:, i : i + 1]
            )
            beside = other[0, i, start:stop, :]
            if has_remote:
                beside = beside + remote[0, i, start:stop, :]
            factor = base + cubic * (value * value)
            if final:
                factor = factor + (
                    sigma[0] * eigen_strain[3 * i]
                    + sigma[1] * eigen_strain[3 * i + 1]
                    + sigma[2] * eigen_strain[3 * i + 2]
                )
            result = (
                value * factor
                + coupling * beside
                + (w_up * upper + w_dn * lower)
                + (w_left * left + w_right * right)
            )
            out[0, i, start:stop, :] = result
            if not final:
                square = result * result
                for c in range(3):
                    sums[c] = sums[c] + square * eigen_strain[3 * i + c]
        if not final:
            for c in range(3):
                out_eigen[c, start:stop, :] = sums[c]


def run_update(places, fields, other, remote, mobility, edges, mob_edges, eigen_strain, extra):
    layers, rows, cols = mobility.shape
    count = fields.shape[1]
    block = min(rows, 4 * STRIP)
    steps = rows // block
    per = block // STRIP
    tops = rows // STRIP - 1
    has_remote = remote is not None
    final = extra is not None

    def spec(shape, index):
        return pl.BlockSpec(shape, index)

    def above(r):
        return jnp.maximum(r * per - 1, 0)

    def below(r):
        return jnp.minimum((r + 1) * per, tops)

    smem = pl.BlockSpec(memory_space=pltpu.SMEM)
    any_space = pl.BlockSpec(memory_space=pl.ANY)
    args = [fields, fields, fields, other]
    specs = [
        spec((1, count, block, cols), lambda r, p: (p[0], 0, r, 0)),
        spec((1, count, STRIP, cols), lambda r, p: (p[0], 0, above(r), 0)),
        spec((1, count, STRIP, cols), lambda r, p: (p[0], 0, below(r), 0)),
        spec((1, count, block, cols), lambda r, p: (p[1], 0, r, 0)),
    ]
    if has_remote:
        args.append(remote)
        specs.append(spec((1, count, block, cols), lambda r, p: (0, 0, r, 0)))
    args += [mobility, mobility, mobility]
    specs += [
        spec((1, block, cols), lambda r, p: (p[2], r, 0)),
        spec((1, STRIP, cols), lambda r, p: (p[2], above(r), 0)),
        spec((1, STRIP, cols), lambda r, p: (p[2], below(r), 0)),
    ]
    for group, at in ((edges, 0), (mob_edges, 2)):
        for rows_edge in group[:2]:
            args.append(rows_edge)
            specs.append(
                spec((1, rows_edge.shape[1], cols), lambda r, p, at=at: (p[at], 0, 0))
            )
        args.append(group[2])
        specs.append(
            spec((1, block, group[2].shape[2]), lambda r, p, at=at: (p[at], r, 0))
        )
    args.append(eigen_strain)
    specs.append(smem)
    out_fields = jax.ShapeDtypeStruct((layers if final else 1, count, rows, cols), jnp.float32)
    field_at = spec(
        (1, count, block, cols), (lambda r, p: (p[2], 0, r, 0)) if final else (lambda r, p: (0, 0, r, 0))
    )
    aliases = {}
    if final:
        signs, macro, stiff, eigen, swaps, held = extra
        args += [signs, macro, stiff, eigen]
        specs += [
            smem,
            smem,
            spec((1, 2, block, cols), lambda r, p: (p[2], 0, r, 0)),
            spec((3, block, cols), lambda r, p: (0, r, 0)),
        ]
        for pair in swaps:
            for value in pair:
                args.append(value)
                specs.append(spec((3, block, cols), lambda r, p: (0, r, 0)))
        if held is not None:
            aliases = {1 + len(args): 0, 2 + len(args): 1}
            args += list(held)
            specs += [any_space, any_space]
        out_shape = (out_fields, jax.ShapeDtypeStruct((layers, 3, rows, cols), jnp.float32))
        out_specs = (field_at, spec((1, 3, block, cols), lambda r, p: (p[2], 0, r, 0)))
    else:
        out_shape = (out_fields, jax.ShapeDtypeStruct((3, rows, cols), jnp.float32))
        out_specs = (field_at, spec((3, block, cols), lambda r, p: (0, r, 0)))

    def kernel(*refs):
        update_kernel(has_remote, final, count, *refs)

    return pl.pallas_call(
        kernel,
        grid_spec=pltpu.PrefetchScalarGridSpec(
            num_scalar_prefetch=1,
            grid=(steps,),
            in_specs=specs,
            out_specs=out_specs,
        ),
        out_shape=out_shape,
        input_output_aliases=aliases,
        compiler_params=pltpu.CompilerParams(vmem_limit_bytes=VMEM_LIMIT),
        name="final_update" if final else "first_update",
    )(places, *args)


def forward_kernel(has_swap, parts, *refs):
    refs = list(refs)
    refs.pop(0)
    signs, macro, stiff, stiff_far, eigen, eigen_far = (refs.pop(0) for _ in range(6))
    swap = (refs.pop(0), refs.pop(0)) if has_swap else None
    high, low, out, flat = refs
    rows = eigen.shape[1]
    sign = signs[0]
    near = []
    far = []
    for c in range(3):
        strain = strain_far = macro[c]
        if has_swap:
            mine = swap[0][c]
            theirs = swap[1][c]
            strain = strain - (theirs + sign * mine)
            strain_far = strain_far - (mine - sign * theirs)
        near.append(strain - eigen[c])
        far.append(strain_far - eigen_far[c])

    def stress(elastic, table):
        lam = table[0, 0]
        shear2 = 2.0 * table[0, 1]
        spread = lam * (elastic[0] + elastic[1])
        return (
            spread + shear2 * elastic[0],
            spread + shear2 * elastic[1],
            shear2 * elastic[2],
        )

    near = stress(near, stiff)
    far = stress(far, stiff_far)
    for c in range(3):
        flat[c * rows : (c + 1) * rows, :] = far[c] + sign * near[c]
    result = dot3((high[0], low[0]), split3(flat[...]), ((1,), (1,)))
    width = result.shape[0] // 2
    part = width // parts
    for q in range(parts):
        for side in range(2):
            at = side * width + q * part
            for c in range(3):
                out[q, side, c] = result[at : at + part, c * rows : (c + 1) * rows]


def run_forward(places, signs, macro, stiff, stiff_far, eigen, eigen_far, swap, waves, parts):
    rows, cols = eigen.shape[1:]
    width = waves[0].shape[1]
    smem = pl.BlockSpec(memory_space=pltpu.SMEM)
    plane = pl.BlockSpec((3, rows, cols), lambda g, p: (0, 0, 0))
    table = pl.BlockSpec((1, 2, rows, cols), lambda g, p: (p[2], 0, 0, 0))
    wave = pl.BlockSpec((1, width, cols), lambda g, p: (0, 0, 0))
    args = [signs, macro, stiff, stiff_far, eigen, eigen_far]
    specs = [smem, smem, table, table, plane, plane]
    if swap is not None:
        args += list(swap)
        specs += [plane, plane]
    args += list(waves)
    specs += [wave, wave]
    shape = (parts, 2, 3, width // (2 * parts), rows)

    def kernel(*refs):
        forward_kernel(swap is not None, parts, *refs)

    return pl.pallas_call(
        kernel,
        grid_spec=pltpu.PrefetchScalarGridSpec(
            num_scalar_prefetch=1,
            grid=(1,),
            in_specs=specs,
            out_specs=pl.BlockSpec(shape, lambda g, p: (0, 0, 0, 0, 0)),
            scratch_shapes=[pltpu.VMEM((3 * rows, cols), jnp.float32)],
        ),
        out_shape=jax.ShapeDtypeStruct(shape, jnp.float32),
        compiler_params=pltpu.CompilerParams(vmem_limit_bytes=VMEM_LIMIT),
        name="forward_columns",
    )(places, *args)


def inverse_kernel(recv, high, low, out, flat):
    parts, _, _, part, rows = recv.shape
    width = parts * part
    for q in range(parts):
        for side in range(2):
            at = side * width + q * part
            for c in range(3):
                flat[at : at + part, c * rows : (c + 1) * rows] = recv[q, side, c]
    result = dot3(split3(flat[...]), (high[0], low[0]), ((0,), (0,)))
    for c in range(3):
        out[c] = result[c * rows : (c + 1) * rows, :]


def run_inverse(recv, waves):
    parts, _, _, part, rows = recv.shape
    _, width, cols = waves[0].shape
    return pl.pallas_call(
        inverse_kernel,
        out_shape=jax.ShapeDtypeStruct((3, rows, cols), jnp.float32),
        scratch_shapes=[pltpu.VMEM((width, 3 * rows), jnp.float32)],
        compiler_params=pltpu.CompilerParams(vmem_limit_bytes=VMEM_LIMIT),
        name="inverse_columns",
    )(recv, *waves)


def rows_kernel(rows_total, cols_total, places, recv, turns, high, low, out, held):
    parts, _, _, part, rows = recv.shape
    span = rows_total // RADIX

    def turn(c):
        return turns[2 * c : 2 * c + 1, :], turns[2 * c + 1 : 2 * c + 2, :]

    def at(c, n):
        start = (c * 3 + n) * part
        return slice(start, start + part)

    def gather(side, n):
        if parts == 1:
            return recv[0, side, n]
        return jnp.concatenate([recv[s, side, n] for s in range(parts)], axis=1)

    for n in range(3):
        real = gather(0, n)
        imag = gather(1, n)
        r = [real[:, a * span : (a + 1) * span] for a in range(RADIX)]
        m = [imag[:, a * span : (a + 1) * span] for a in range(RADIX)]
        r02, r13, d02, d13 = r[0] + r[2], r[1] + r[3], r[0] - r[2], r[1] - r[3]
        m02, m13, e02, e13 = m[0] + m[2], m[1] + m[3], m[0] - m[2], m[1] - m[3]
        mixed = (
            (r02 + r13, m02 + m13),
            (d02 + e13, e02 - d13),
            (r02 - r13, m02 - m13),
            (d02 - e13, e02 + d13),
        )
        for c in range(RADIX):
            x, y = mixed[c]
            if c:
                cosine, sine = turn(c)
                x, y = x * cosine + y * sine, y * cosine - x * sine
            held[at(c, n), :span] = x
            held[at(c, n), span:] = y
    wave = (high[...], low[...])
    held[...] = dot3(split3(held[...]), wave, ((1,), (0,)))

    lanes = lax.broadcasted_iota(jnp.int32, (part, 2 * span), 1)
    lanes = jnp.where(lanes >= span, lanes - span, lanes)
    lines = lax.broadcasted_iota(jnp.int32, (part, 2 * span), 0)
    freq_col = 2 * (places[3] * part + lines) + places[4]
    signed_col = freq_col.astype(jnp.float32)
    scale = jnp.where(freq_col == 0, 1.0, 2.0) * (1.0 / (rows_total * cols_total))
    for c in range(RADIX):
        freq_row = RADIX * lanes + c
        signed_row = jnp.where(
            freq_row >= rows_total // 2, freq_row - rows_total, freq_row
        ).astype(jnp.float32)
        radius = signed_row * signed_row + signed_col * signed_col
        keep = (freq_row != rows_total // 2) & (freq_col != cols_total // 2)
        inverse = jnp.where(keep & (radius > 0.0), 1.0 / jnp.maximum(radius, 1.0), 0.0)
        n11 = signed_row * signed_row * inverse
        n12 = signed_row * signed_col * inverse
        n22 = signed_col * signed_col * inverse
        s_rr = held[at(c, 0), :]
        s_cc = held[at(c, 1), :]
        s_rc = held[at(c, 2), :]
        along_r = s_rr * n11 + s_rc * n12
        along_c = s_rc * n12 + s_cc * n22
        normal = BETA_REF * (along_r + along_c)
        cross = 0.5 * (n12 * (s_rr + s_cc) + s_rc * (n11 + n22))
        held[at(c, 0), :] = scale * (along_r * (1.0 / SHEAR_REF) - n11 * normal)
        held[at(c, 1), :] = scale * (along_c * (1.0 / SHEAR_REF) - n22 * normal)
        held[at(c, 2), :] = scale * (cross * (1.0 / SHEAR_REF) - n12 * normal)
    held[...] = dot3(split3(held[...]), wave, ((1,), (1,)))
    for n in range(3):
        v = []
        for c in range(RADIX):
            x = held[at(c, n), :span]
            y = held[at(c, n), span:]
            if c:
                cosine, sine = turn(c)
                x, y = x * cosine - y * sine, y * cosine + x * sine
            v.append((x, y))
        r02, r13 = v[0][0] + v[2][0], v[1][0] + v[3][0]
        d02, d13 = v[0][0] - v[2][0], v[1][0] - v[3][0]
        m02, m13 = v[0][1] + v[2][1], v[1][1] + v[3][1]
        e02, e13 = v[0][1] - v[2][1], v[1][1] - v[3][1]
        real = jnp.concatenate([r02 + r13, d02 - e13, r02 - r13, d02 + e13], axis=1)
        imag = jnp.concatenate([m02 + m13, e02 + d13, m02 - m13, e02 - d13], axis=1)
        for s in range(parts):
            out[s, 0, n] = real[:, s * rows : (s + 1) * rows]
            out[s, 1, n] = imag[:, s * rows : (s + 1) * rows]


def row_wave(span):
    ids = np.arange(span)
    angle = (np.outer(ids, ids) % span) * (2.0 * math.pi / span)
    cosine, sine = np.cos(angle), np.sin(angle)
    full = np.block([[cosine, -sine], [sine, cosine]]).astype(np.float32)
    high = full.astype(jnp.bfloat16)
    low = (full - high.astype(np.float32)).astype(jnp.bfloat16)
    turns = []
    for c in range(RADIX):
        angle = ids * c * (2.0 * math.pi / (RADIX * span))
        turns += [np.cos(angle), np.sin(angle)]
    return np.stack(turns).astype(np.float32), high, low


def run_rows(places, recv, tables, rows_total, cols_total):
    parts, _, _, part, rows = recv.shape
    dense = rows % 128 == 0
    if not dense:
        recv = jnp.transpose(recv, (1, 2, 3, 0, 4)).reshape(1, 2, 3, part, rows_total)
    span = rows_total // RADIX

    def kernel(*refs):
        rows_kernel(rows_total, cols_total, *refs)

    whole = pl.BlockSpec(memory_space=pltpu.VMEM)
    out = pl.pallas_call(
        kernel,
        in_specs=[pl.BlockSpec(memory_space=pltpu.SMEM), whole, whole, whole, whole],
        out_specs=whole,
        out_shape=jax.ShapeDtypeStruct(recv.shape, jnp.float32),
        scratch_shapes=[pltpu.VMEM((RADIX * 3 * part, 2 * span), jnp.float32)],
        compiler_params=pltpu.CompilerParams(vmem_limit_bytes=VMEM_LIMIT),
        name="row_lines",
    )(places, recv, *tables)
    if not dense:
        out = jnp.transpose(out.reshape(2, 3, part, parts, rows), (3, 0, 1, 2, 4))
    return out


def table_lookup(labels, values_table, entries):
    result = jnp.zeros(labels.shape, jnp.float32)
    for entry in range(entries):
        result = jnp.where(labels == entry, values_table[entry], result)
    return result


def column_waves(freqs, ids, length):
    product = freqs[:, None] * ids[None, :] % length
    angle = product.astype(jnp.float32) * (2.0 * math.pi / length)
    full = jnp.concatenate([jnp.cos(angle), -jnp.sin(angle)], axis=0)[None]
    rounded = lax.reduce_precision(full, 8, 7)
    return rounded.astype(jnp.bfloat16), (full - rounded).astype(jnp.bfloat16)


def body(
    order_field,
    grain_label,
    phase_label,
    grain_mobility,
    stiff_index,
    stiff_table,
    eigen_strain,
    macro_strain,
):
    layers, count, rows, cols = order_field.shape
    parts = lax.axis_size("row")
    if lax.axis_size("grp") != 2 or layers != 2 or lax.axis_size("col") != 2:
        raise ValueError("unsupported split")
    group = lax.axis_index("grp").astype(jnp.int32)
    row_place = lax.axis_index("row").astype(jnp.int32)
    col_place = lax.axis_index("col").astype(jnp.int32)
    rows_total = rows * parts
    cols_total = cols * 2
    inner = group
    outer = 1 - group
    swap_pairs = [(0, 1), (1, 0)]
    ring_up = [(i, (i + 1) % parts) for i in range(parts)]
    ring_down = [(j, i) for i, j in ring_up]

    def swap_cols(value):
        return lax.ppermute(value, "col", swap_pairs)

    def swap_layers(value):
        return lax.ppermute(value, "grp", swap_pairs)

    remote_field = swap_layers(lax.dynamic_slice_in_dim(order_field, outer, 1, 0))

    mobility = table_lookup(grain_label, grain_mobility, grain_mobility.shape[0])
    sets = stiff_table.shape[0]
    lambda_phase = table_lookup(stiff_index, stiff_table[:, 0], sets)
    shear_phase = table_lookup(stiff_index, stiff_table[:, 1], sets)
    phases = stiff_index.shape[0]
    stiff = jnp.stack(
        [
            table_lookup(phase_label, lambda_phase, phases),
            table_lookup(phase_label, shear_phase, phases),
        ],
        axis=1,
    )

    def edges_of(fields, more=None):
        top = fields[:, :, 0, :]
        bottom = fields[:, :, rows - 1, :]
        sides = jnp.stack([fields[:, :, :, 0], fields[:, :, :, cols - 1]], axis=1)
        if more is not None:
            top = jnp.concatenate([top, more[:, None, 0, :]], axis=1)
            bottom = jnp.concatenate([bottom, more[:, None, rows - 1, :]], axis=1)
            more_sides = jnp.stack([more[:, :, 0], more[:, :, cols - 1]], axis=1)
            sides = jnp.concatenate([sides, more_sides[:, :, None]], axis=2)
        up = lax.ppermute(bottom, "row", ring_up)
        down = lax.ppermute(top, "row", ring_down)
        sides = swap_cols(sides)
        lead = sides.shape[0]
        sides = jnp.transpose(sides.reshape(lead, -1, rows), (0, 2, 1))
        return up, down, sides

    edges = edges_of(order_field, mobility)
    stiff_far = swap_cols(stiff)
    signs = (1 - 2 * col_place).astype(jnp.float32)[None]
    strain_table = eigen_strain.reshape(-1)
    waves = column_waves(
        2 * jnp.arange(cols_total // 4, dtype=jnp.int32) + col_place,
        jnp.arange(cols, dtype=jnp.int32),
        cols_total,
    )
    tables = row_wave(rows_total // RADIX)

    def places(phi_at, other_at, layer):
        zero = jnp.zeros((), jnp.int32)
        return jnp.stack([zero + phi_at, zero + other_at, layer, row_place, col_place])

    def exchange(value):
        return lax.all_to_all(value, "row", split_axis=0, concat_axis=0, tiled=True)

    def first(layer, beside, remote):
        return run_update(
            places(layer, beside, layer),
            order_field,
            order_field,
            remote,
            mobility,
            edges,
            edges,
            strain_table,
            None,
        )

    def chain(layer, eigen):
        here = places(0, 0, layer)
        eigen_far = swap_cols(eigen)
        swaps = []
        for _ in range(ITERS):
            sent = run_forward(
                here,
                signs,
                macro_strain,
                stiff,
                stiff_far,
                eigen,
                eigen_far,
                swaps[-1] if swaps else None,
                waves,
                parts,
            )
            lines = run_rows(here, exchange(sent), tables, rows_total, cols_total)
            mine = run_inverse(exchange(lines), waves)
            swaps.append((mine, swap_cols(mine)))
        return swaps

    middle_inner, eigen_inner = first(inner, outer, None)
    swaps_inner = chain(inner, eigen_inner)
    middle_outer, eigen_outer = first(outer, inner, remote_field)
    remote_middle = swap_layers(middle_outer)
    edges_inner = edges_of(middle_inner)
    edges_outer = edges_of(middle_outer)
    swaps_outer = chain(outer, eigen_outer)

    def last(layer, fields, beside, remote, own_edges, eigen, swaps, held):
        return run_update(
            places(0, 0, layer),
            fields,
            beside,
            remote,
            mobility,
            own_edges,
            edges,
            strain_table,
            (signs, macro_strain, stiff, eigen, swaps, held),
        )

    held = last(inner, middle_inner, middle_outer, None, edges_inner, eigen_inner, swaps_inner, None)
    return last(
        outer,
        middle_outer,
        middle_inner,
        remote_middle,
        edges_outer,
        eigen_outer,
        swaps_outer,
        held,
    )


def solution(mesh):
    return jax.shard_map(
        body,
        mesh=mesh,
        in_specs=(
            P("grp", None, "row", "col"),
            P("grp", "row", "col"),
            P("grp", "row", "col"),
            P(),
            P(),
            P(),
            P(),
            P(),
        ),
        out_specs=(P("grp", None, "row", "col"), P("grp", None, "row", "col")),
        check_vma=False,
    )
```

```python
import math

import jax
import jax.numpy as jnp
import numpy as np
from jax import lax
from jax.experimental import pallas as pl
from jax.experimental.pallas import tpu as pltpu
from jax.sharding import PartitionSpec as P


ITERS = 2
GAMMA_MIX = 1.5
KAPPA_GRAD = 1.0
STEP_TIME = 0.1
LAYER_COUPLE = 0.5
LAMBDA_REF = 1.25
SHEAR_REF = 1.25
BETA_REF = (LAMBDA_REF + SHEAR_REF) / (SHEAR_REF * (LAMBDA_REF + 2.0 * SHEAR_REF))
STRIP = 8
LANES = 128
RADIX = 4
VMEM_LIMIT = 56 * 1024 * 1024


def split3(value):
    high = value.astype(jnp.bfloat16)
    low = (value - high.astype(jnp.float32)).astype(jnp.bfloat16)
    return high, low


def dot3(left, right, dims):
    left_high, left_low = left
    right_high, right_low = right

    def product(a, b):
        return lax.dot_general(a, b, (dims, ((), ())), preferred_element_type=jnp.float32)

    return product(left_high, right_high) + (
        product(left_high, right_low) + product(left_low, right_high)
    )


def shift_rows(value, before, after):
    place = lax.broadcasted_iota(jnp.int32, value.shape, 0)
    size = value.shape[0]
    upper = jnp.where(place == 0, before, pltpu.roll(value, 1, 0))
    lower = jnp.where(place == size - 1, after, pltpu.roll(value, size - 1, 0))
    return upper, lower


def shift_cols(value, before, after):
    size = value.shape[1]
    lanes = min(size, LANES)
    place = lax.broadcasted_iota(jnp.int32, (value.shape[0], lanes), 1)
    left = pltpu.roll(value, 1, 1)
    right = pltpu.roll(value, size - 1, 1)
    head = jnp.where(place == 0, before, left[:, :lanes])
    tail = jnp.where(place == lanes - 1, after, right[:, size - lanes :])
    if size == lanes:
        return head, tail
    return (
        jnp.concatenate([head, left[:, lanes:]], axis=1),
        jnp.concatenate([right[:, : size - lanes], tail], axis=1),
    )


def put_lane(packed, lane, column):
    place = lax.broadcasted_iota(jnp.int32, packed.shape, 1)
    return jnp.where(place == lane, column, packed)


def prepare_kernel(
    grain, phase, top_rows, bottom_rows, left, right, speeds, index, table,
    mobility, stiff, edge_up, edge_dn, edge_col,
):
    count, rows = left.shape[1], left.shape[2]
    width = left.shape[3]
    labels = grain[0]
    speed = jnp.zeros(labels.shape, jnp.float32)
    for entry in range(speeds.shape[0]):
        speed = jnp.where(labels == entry, speeds[entry], speed)
    mobility[0] = speed
    labels = phase[0]
    lam = jnp.zeros(labels.shape, jnp.float32)
    shear = jnp.zeros(labels.shape, jnp.float32)
    for entry in range(index.shape[0]):
        match = labels == entry
        lam = jnp.where(match, table[index[entry], 0], lam)
        shear = jnp.where(match, table[index[entry], 1], shear)
    stiff[0, 0] = lam
    stiff[0, 1] = shear
    packed = jnp.zeros((rows, LANES), jnp.float32)
    for i in range(count):
        packed = put_lane(packed, i, left[0, i, :, 0:1])
        packed = put_lane(packed, count + 1 + i, right[0, i, :, width - 1 : width])
    packed = put_lane(packed, count, speed[:, 0:1])
    packed = put_lane(packed, 2 * count + 1, speed[:, speed.shape[1] - 1 :])
    edge_col[0] = packed[:, : 2 * count + 2]
    block = pl.program_id(1)

    @pl.when(block == 0)
    def _():
        for i in range(count):
            edge_up[0, i : i + 1, :] = top_rows[0, i, 0:1, :]
            edge_dn[0, i : i + 1, :] = bottom_rows[0, i, STRIP - 1 : STRIP, :]
        edge_up[0, count : count + 1, :] = speed[0:1, :]

    @pl.when(block == pl.num_programs(1) - 1)
    def _():
        edge_dn[0, count : count + 1, :] = speed[rows - 1 : rows, :]


def run_prepare(order_field, grain_label, phase_label, grain_mobility, stiff_index, stiff_table):
    layers, count, rows, cols = order_field.shape
    block = min(rows, 8 * STRIP)
    width = min(cols, LANES)
    smem = pl.BlockSpec(memory_space=pltpu.SMEM)
    shape = jax.ShapeDtypeStruct
    return pl.pallas_call(
        prepare_kernel,
        grid=(layers, rows // block),
        in_specs=[
            pl.BlockSpec((1, block, cols), lambda l, r: (l, r, 0)),
            pl.BlockSpec((1, block, cols), lambda l, r: (l, r, 0)),
            pl.BlockSpec((1, count, STRIP, cols), lambda l, r: (l, 0, 0, 0)),
            pl.BlockSpec((1, count, STRIP, cols), lambda l, r: (l, 0, rows // STRIP - 1, 0)),
            pl.BlockSpec((1, count, block, width), lambda l, r: (l, 0, r, 0)),
            pl.BlockSpec((1, count, block, width), lambda l, r: (l, 0, r, cols // width - 1)),
            smem,
            smem,
            smem,
        ],
        out_specs=(
            pl.BlockSpec((1, block, cols), lambda l, r: (l, r, 0)),
            pl.BlockSpec((1, 2, block, cols), lambda l, r: (l, 0, r, 0)),
            pl.BlockSpec((1, count + 1, cols), lambda l, r: (l, 0, 0)),
            pl.BlockSpec((1, count + 1, cols), lambda l, r: (l, 0, 0)),
            pl.BlockSpec((1, block, 2 * count + 2), lambda l, r: (l, r, 0)),
        ),
        out_shape=(
            shape((layers, rows, cols), jnp.float32),
            shape((layers, 2, rows, cols), jnp.float32),
            shape((layers, count + 1, cols), jnp.float32),
            shape((layers, count + 1, cols), jnp.float32),
            shape((layers, rows, 2 * count + 2), jnp.float32),
        ),
        compiler_params=pltpu.CompilerParams(vmem_limit_bytes=VMEM_LIMIT),
        name="prepare",
    )(
        grain_label, phase_label, order_field, order_field, order_field, order_field,
        grain_mobility, stiff_index, stiff_table,
    )


def pack_sides(fields, out_col):
    count, rows, cols = fields.shape[1:]
    packed = jnp.zeros((rows, LANES), jnp.float32)
    for i in range(count):
        packed = put_lane(packed, i, fields[0, i, :, 0:1])
        packed = put_lane(packed, count + i, fields[0, i, :, cols - 1 : cols])
    out_col[0] = packed[:, : 2 * count]


def emit_rim(fields, out_up, out_dn, out_col):
    count, rows, _ = fields.shape[1:]
    pack_sides(fields, out_col)

    @pl.when(pl.program_id(0) == 0)
    def _():
        for i in range(count):
            out_up[0, i : i + 1, :] = fields[0, i, 0:1, :]

    @pl.when(pl.program_id(0) == pl.num_programs(0) - 1)
    def _():
        for i in range(count):
            out_dn[0, i : i + 1, :] = fields[0, i, rows - 1 : rows, :]


def stencil_kernel(has_remote, emit, waits, count, *refs):
    refs = list(refs)
    refs.pop(0)
    phi, phi_up, phi_dn, other = (refs.pop(0) for _ in range(4))
    remote = refs.pop(0) if has_remote else None
    mob, mob_up, mob_dn = (refs.pop(0) for _ in range(3))
    edge_up, edge_dn, edge_col = (refs.pop(0) for _ in range(3))
    mob_edge_up, mob_edge_dn, mob_edge_col = (refs.pop(0) for _ in range(3))
    eigen_strain = refs.pop(0)
    del refs[:waits]
    out = refs.pop(0)
    if emit:
        out_eigen, out_up, out_dn, out_col = refs
    block = pl.program_id(0)
    first = block == 0
    last = block == pl.num_programs(0) - 1
    rows, _ = phi.shape[2:]
    strips = rows // STRIP
    side = edge_col.shape[2] // 2
    mob_side = mob_edge_col.shape[2] // 2

    def strip_body(strip, carry):
        start = pl.multiple_of(strip * STRIP, STRIP)
        here = pl.ds(start, STRIP)
        at_top = strip == 0
        at_bottom = strip == strips - 1

        def before_after(main, up, dn, edge_before, edge_after):
            before = jnp.where(
                at_top,
                jnp.where(first, edge_before, up),
                main(pl.ds(jnp.maximum(start - 1, 0), 1)),
            )
            after = jnp.where(
                at_bottom,
                jnp.where(last, edge_after, dn),
                main(pl.ds(jnp.minimum(start + STRIP, rows - 1), 1)),
            )
            return before, after

        m = mob[0, here, :]
        before, after = before_after(
            lambda r: mob[0, r, :],
            mob_up[0, STRIP - 1 : STRIP, :],
            mob_dn[0, 0:1, :],
            mob_edge_up[0, count : count + 1, :],
            mob_edge_dn[0, count : count + 1, :],
        )
        m_up, m_dn = shift_rows(m, before, after)
        m_edges = mob_edge_col[0, here, :]
        m_left, m_right = shift_cols(
            m,
            m_edges[:, mob_side + count : mob_side + count + 1],
            m_edges[:, count : count + 1],
        )
        half_step = 0.5 * STEP_TIME * KAPPA_GRAD
        w_up = half_step * (m + m_up)
        w_dn = half_step * (m + m_dn)
        w_left = half_step * (m + m_left)
        w_right = half_step * (m + m_right)
        total = jnp.zeros_like(m)
        for i in range(count):
            value = phi[0, i, here, :]
            total = total + value * value
        scaled = STEP_TIME * m
        base = (
            1.0
            - (w_up + w_dn + w_left + w_right)
            + scaled * ((1.0 - 2.0 * LAYER_COUPLE) - 2.0 * GAMMA_MIX * total)
        )
        coupling = LAYER_COUPLE * scaled
        cubic = (2.0 * GAMMA_MIX - 1.0) * scaled
        if emit:
            sums = [jnp.zeros_like(m) for _ in range(3)]
        edges = edge_col[0, here, :]
        for i in range(count):
            value = phi[0, i, here, :]
            before, after = before_after(
                lambda r: phi[0, i, r, :],
                phi_up[0, i, STRIP - 1 : STRIP, :],
                phi_dn[0, i, 0:1, :],
                edge_up[0, i : i + 1, :],
                edge_dn[0, i : i + 1, :],
            )
            upper, lower = shift_rows(value, before, after)
            left, right = shift_cols(
                value, edges[:, side + i : side + i + 1], edges[:, i : i + 1]
            )
            beside = other[0, i, here, :]
            if has_remote:
                beside = beside + remote[0, i, here, :]
            result = (
                value * (base + cubic * (value * value))
                + coupling * beside
                + (w_up * upper + w_dn * lower)
                + (w_left * left + w_right * right)
            )
            out[0, i, here, :] = result
            if emit:
                square = result * result
                for c in range(3):
                    sums[c] = sums[c] + square * eigen_strain[3 * i + c]
        if emit:
            for c in range(3):
                out_eigen[c, here, :] = sums[c]
        return carry

    lax.fori_loop(0, strips, strip_body, 0)
    if emit:
        emit_rim(out, out_up, out_dn, out_col)


def rim_outputs(count, rows, cols, block):
    shape = jax.ShapeDtypeStruct
    shapes = (
        shape((1, count, rows, cols), jnp.float32),
        shape((3, rows, cols), jnp.float32),
        shape((1, count, cols), jnp.float32),
        shape((1, count, cols), jnp.float32),
        shape((1, rows, 2 * count), jnp.float32),
    )
    specs = (
        pl.BlockSpec((1, count, block, cols), lambda r, p: (0, 0, r, 0)),
        pl.BlockSpec((3, block, cols), lambda r, p: (0, r, 0)),
        pl.BlockSpec((1, count, cols), lambda r, p: (0, 0, 0)),
        pl.BlockSpec((1, count, cols), lambda r, p: (0, 0, 0)),
        pl.BlockSpec((1, block, 2 * count), lambda r, p: (0, r, 0)),
    )
    return shapes, specs


def any_specs(values):
    return [pl.BlockSpec(memory_space=pl.ANY) for _ in values]


def run_stencil(
    places, fields, other, remote, mobility, edges, mob_edges, eigen_strain, emit, after=()
):
    _, rows, cols = mobility.shape
    count = fields.shape[1]
    block = min(rows, 4 * STRIP)
    per = block // STRIP
    tops = rows // STRIP - 1
    has_remote = remote is not None
    spec = pl.BlockSpec

    def above(r):
        return jnp.maximum(r * per - 1, 0)

    def below(r):
        return jnp.minimum((r + 1) * per, tops)

    args = [fields, fields, fields, other]
    specs = [
        spec((1, count, block, cols), lambda r, p: (p[0], 0, r, 0)),
        spec((1, count, STRIP, cols), lambda r, p: (p[0], 0, above(r), 0)),
        spec((1, count, STRIP, cols), lambda r, p: (p[0], 0, below(r), 0)),
        spec((1, count, block, cols), lambda r, p: (p[1], 0, r, 0)),
    ]
    if has_remote:
        args.append(remote)
        specs.append(spec((1, count, block, cols), lambda r, p: (0, 0, r, 0)))
    args += [mobility, mobility, mobility]
    specs += [
        spec((1, block, cols), lambda r, p: (p[2], r, 0)),
        spec((1, STRIP, cols), lambda r, p: (p[2], above(r), 0)),
        spec((1, STRIP, cols), lambda r, p: (p[2], below(r), 0)),
    ]
    for group, at in ((edges, 0), (mob_edges, 2)):
        for rows_edge in group[:2]:
            args.append(rows_edge)
            specs.append(
                spec((1, rows_edge.shape[1], cols), lambda r, p, at=at: (p[at], 0, 0))
            )
        args.append(group[2])
        specs.append(
            spec((1, block, group[2].shape[2]), lambda r, p, at=at: (p[at], r, 0))
        )
    args += [eigen_strain, *after]
    specs += [spec(memory_space=pltpu.SMEM), *any_specs(after)]
    out_shape, out_specs = rim_outputs(count, rows, cols, block)
    if not emit:
        out_shape, out_specs = out_shape[0], out_specs[0]

    def kernel(*refs):
        stencil_kernel(has_remote, emit, len(after), count, *refs)

    return pl.pallas_call(
        kernel,
        grid_spec=pltpu.PrefetchScalarGridSpec(
            num_scalar_prefetch=1,
            grid=(rows // block,),
            in_specs=specs,
            out_specs=out_specs,
        ),
        out_shape=out_shape,
        compiler_params=pltpu.CompilerParams(vmem_limit_bytes=VMEM_LIMIT),
        name="stencil",
    )(places, *args)


def finish_kernel(waits, places, partial, remote, mob, eigen_strain, *refs):
    out, out_eigen, out_up, out_dn, out_col = refs[waits:]
    count, rows = out.shape[1:3]
    for start in range(0, rows, STRIP):
        here = slice(start, start + STRIP)
        coupling = (LAYER_COUPLE * STEP_TIME) * mob[0, here, :]
        sums = [jnp.zeros_like(coupling) for _ in range(3)]
        for i in range(count):
            result = partial[0, i, here, :] + coupling * remote[0, i, here, :]
            out[0, i, here, :] = result
            square = result * result
            for c in range(3):
                sums[c] = sums[c] + square * eigen_strain[3 * i + c]
        for c in range(3):
            out_eigen[c, here, :] = sums[c]
    emit_rim(out, out_up, out_dn, out_col)


def run_finish(places, partial, remote, mobility, eigen_strain, after):
    _, rows, cols = mobility.shape
    count = partial.shape[1]
    block = min(rows, 4 * STRIP)
    field = pl.BlockSpec((1, count, block, cols), lambda r, p: (0, 0, r, 0))
    out_shape, out_specs = rim_outputs(count, rows, cols, block)

    def kernel(*refs):
        finish_kernel(len(after), *refs)

    return pl.pallas_call(
        kernel,
        grid_spec=pltpu.PrefetchScalarGridSpec(
            num_scalar_prefetch=1,
            grid=(rows // block,),
            in_specs=[
                field,
                field,
                pl.BlockSpec((1, block, cols), lambda r, p: (p[2], r, 0)),
                pl.BlockSpec(memory_space=pltpu.SMEM),
                *any_specs(after),
            ],
            out_specs=out_specs,
        ),
        out_shape=out_shape,
        compiler_params=pltpu.CompilerParams(vmem_limit_bytes=VMEM_LIMIT),
        name="finish",
    )(places, partial, remote, mobility, eigen_strain, *after)


def drive_kernel(places, pre, phi, mob, stiff, eigen, eigen_strain, signs, macro, *refs):
    swaps = [(refs[2 * k], refs[2 * k + 1]) for k in range(ITERS)]
    out, out_strain = refs[-2:]
    count, rows = phi.shape[1:3]
    sign = signs[0]
    for start in range(0, rows, STRIP):
        here = slice(start, start + STRIP)
        lam = stiff[0, 0, here, :]
        shear2 = 2.0 * stiff[0, 1, here, :]
        elastic = []
        for c in range(3):
            strain = macro[c]
            for mine, theirs in swaps:
                strain = strain - (theirs[c, here, :] + sign * mine[c, here, :])
            out_strain[0, c, here, :] = strain
            elastic.append(strain - eigen[c, here, :])
        spread = lam * (elastic[0] + elastic[1])
        push = (2.0 * STEP_TIME) * mob[0, here, :]
        sigma = (
            push * (spread + shear2 * elastic[0]),
            push * (spread + shear2 * elastic[1]),
            push * (2.0 * shear2 * elastic[2]),
        )
        for i in range(count):
            force = (
                sigma[0] * eigen_strain[3 * i]
                + sigma[1] * eigen_strain[3 * i + 1]
                + sigma[2] * eigen_strain[3 * i + 2]
            )
            out[0, i, here, :] = pre[0, i, here, :] + phi[0, i, here, :] * force


def run_drive(places, pre, fields, mobility, stiff, eigen, eigen_strain, signs, macro, swaps, held):
    layers, rows, cols = mobility.shape
    count = fields.shape[1]
    block = min(rows, 4 * STRIP)
    smem = pl.BlockSpec(memory_space=pltpu.SMEM)
    field = pl.BlockSpec((1, count, block, cols), lambda r, p: (0, 0, r, 0))
    plane = pl.BlockSpec((3, block, cols), lambda r, p: (0, r, 0))
    args = [pre, fields, mobility, stiff, eigen, eigen_strain, signs, macro]
    specs = [
        field,
        field,
        pl.BlockSpec((1, block, cols), lambda r, p: (p[2], r, 0)),
        pl.BlockSpec((1, 2, block, cols), lambda r, p: (p[2], 0, r, 0)),
        plane,
        smem,
        smem,
        smem,
    ]
    for pair in swaps:
        args += list(pair)
        specs += [plane, plane]
    aliases = {}
    if held is not None:
        aliases = {1 + len(args): 0, 2 + len(args): 1}
        args += list(held)
        specs += any_specs(held)
    return pl.pallas_call(
        drive_kernel,
        grid_spec=pltpu.PrefetchScalarGridSpec(
            num_scalar_prefetch=1,
            grid=(rows // block,),
            in_specs=specs,
            out_specs=(
                pl.BlockSpec((1, count, block, cols), lambda r, p: (p[2], 0, r, 0)),
                pl.BlockSpec((1, 3, block, cols), lambda r, p: (p[2], 0, r, 0)),
            ),
        ),
        out_shape=(
            jax.ShapeDtypeStruct((layers, count, rows, cols), jnp.float32),
            jax.ShapeDtypeStruct((layers, 3, rows, cols), jnp.float32),
        ),
        input_output_aliases=aliases,
        compiler_params=pltpu.CompilerParams(vmem_limit_bytes=VMEM_LIMIT),
        name="drive",
    )(places, *args)


def forward_kernel(has_swap, parts, waits, *refs):
    refs = list(refs)
    refs.pop(0)
    signs, macro, stiff, stiff_far, eigen, eigen_far = (refs.pop(0) for _ in range(6))
    swap = (refs.pop(0), refs.pop(0)) if has_swap else None
    high, low = refs.pop(0), refs.pop(0)
    out, flat = refs[waits:]
    rows = eigen.shape[1]
    sign = signs[0]
    near = []
    far = []
    for c in range(3):
        strain = strain_far = macro[c]
        if has_swap:
            mine = swap[0][c]
            theirs = swap[1][c]
            strain = strain - (theirs + sign * mine)
            strain_far = strain_far - (mine - sign * theirs)
        near.append(strain - eigen[c])
        far.append(strain_far - eigen_far[c])

    def stress(elastic, table):
        lam = table[0, 0]
        shear2 = 2.0 * table[0, 1]
        spread = lam * (elastic[0] + elastic[1])
        return (
            spread + shear2 * elastic[0],
            spread + shear2 * elastic[1],
            shear2 * elastic[2],
        )

    near = stress(near, stiff)
    far = stress(far, stiff_far)
    for c in range(3):
        flat[c * rows : (c + 1) * rows, :] = far[c] + sign * near[c]
    result = dot3((high[0], low[0]), split3(flat[...]), ((1,), (1,)))
    width = result.shape[0] // 2
    part = width // parts
    for q in range(parts):
        for side in range(2):
            at = side * width + q * part
            for c in range(3):
                out[q, side, c] = result[at : at + part, c * rows : (c + 1) * rows]


def run_forward(places, signs, macro, stiff, stiff_far, eigen, eigen_far, swap, waves, parts, after):
    rows, cols = eigen.shape[1:]
    width = waves[0].shape[1]
    smem = pl.BlockSpec(memory_space=pltpu.SMEM)
    plane = pl.BlockSpec((3, rows, cols), lambda g, p: (0, 0, 0))
    table = pl.BlockSpec((1, 2, rows, cols), lambda g, p: (p[2], 0, 0, 0))
    wave = pl.BlockSpec((1, width, cols), lambda g, p: (0, 0, 0))
    args = [signs, macro, stiff, stiff_far, eigen, eigen_far]
    specs = [smem, smem, table, table, plane, plane]
    if swap is not None:
        args += list(swap)
        specs += [plane, plane]
    args += list(waves)
    specs += [wave, wave]
    args += list(after)
    specs += any_specs(after)
    shape = (parts, 2, 3, width // (2 * parts), rows)

    def kernel(*refs):
        forward_kernel(swap is not None, parts, len(after), *refs)

    return pl.pallas_call(
        kernel,
        grid_spec=pltpu.PrefetchScalarGridSpec(
            num_scalar_prefetch=1,
            grid=(1,),
            in_specs=specs,
            out_specs=pl.BlockSpec(shape, lambda g, p: (0, 0, 0, 0, 0)),
            scratch_shapes=[pltpu.VMEM((3 * rows, cols), jnp.float32)],
        ),
        out_shape=jax.ShapeDtypeStruct(shape, jnp.float32),
        compiler_params=pltpu.CompilerParams(vmem_limit_bytes=VMEM_LIMIT),
        name="forward_columns",
    )(places, *args)


def inverse_kernel(recv, high, low, *refs):
    out, flat = refs[-2:]
    parts, _, _, part, rows = recv.shape
    width = parts * part
    for q in range(parts):
        for side in range(2):
            at = side * width + q * part
            for c in range(3):
                flat[at : at + part, c * rows : (c + 1) * rows] = recv[q, side, c]
    result = dot3(split3(flat[...]), (high[0], low[0]), ((0,), (0,)))
    for c in range(3):
        out[c] = result[c * rows : (c + 1) * rows, :]


def run_inverse(recv, waves, after):
    _, _, _, _, rows = recv.shape
    _, width, cols = waves[0].shape
    whole = pl.BlockSpec(memory_space=pltpu.VMEM)
    return pl.pallas_call(
        inverse_kernel,
        in_specs=[whole, whole, whole, *any_specs(after)],
        out_specs=whole,
        out_shape=jax.ShapeDtypeStruct((3, rows, cols), jnp.float32),
        scratch_shapes=[pltpu.VMEM((width, 3 * rows), jnp.float32)],
        compiler_params=pltpu.CompilerParams(vmem_limit_bytes=VMEM_LIMIT),
        name="inverse_columns",
    )(recv, *waves, *after)


def rows_kernel(rows_total, cols_total, places, recv, turns, high, low, *refs):
    out, held = refs[-2:]
    parts, _, _, part, rows = recv.shape
    span = rows_total // RADIX

    def turn(c):
        return turns[2 * c : 2 * c + 1, :], turns[2 * c + 1 : 2 * c + 2, :]

    def at(c, n):
        start = (c * 3 + n) * part
        return slice(start, start + part)

    def gather(side, n):
        if parts == 1:
            return recv[0, side, n]
        return jnp.concatenate([recv[s, side, n] for s in range(parts)], axis=1)

    for n in range(3):
        real = gather(0, n)
        imag = gather(1, n)
        r = [real[:, a * span : (a + 1) * span] for a in range(RADIX)]
        m = [imag[:, a * span : (a + 1) * span] for a in range(RADIX)]
        r02, r13, d02, d13 = r[0] + r[2], r[1] + r[3], r[0] - r[2], r[1] - r[3]
        m02, m13, e02, e13 = m[0] + m[2], m[1] + m[3], m[0] - m[2], m[1] - m[3]
        mixed = (
            (r02 + r13, m02 + m13),
            (d02 + e13, e02 - d13),
            (r02 - r13, m02 - m13),
            (d02 - e13, e02 + d13),
        )
        for c in range(RADIX):
            x, y = mixed[c]
            if c:
                cosine, sine = turn(c)
                x, y = x * cosine + y * sine, y * cosine - x * sine
            held[at(c, n), :span] = x
            held[at(c, n), span:] = y
    wave = (high[...], low[...])
    held[...] = dot3(split3(held[...]), wave, ((1,), (0,)))

    lanes = lax.broadcasted_iota(jnp.int32, (part, 2 * span), 1)
    lanes = jnp.where(lanes >= span, lanes - span, lanes)
    lines = lax.broadcasted_iota(jnp.int32, (part, 2 * span), 0)
    freq_col = 2 * (places[3] * part + lines) + places[4]
    signed_col = freq_col.astype(jnp.float32)
    scale = jnp.where(freq_col == 0, 1.0, 2.0) * (1.0 / (rows_total * cols_total))
    for c in range(RADIX):
        freq_row = RADIX * lanes + c
        signed_row = jnp.where(
            freq_row >= rows_total // 2, freq_row - rows_total, freq_row
        ).astype(jnp.float32)
        radius = signed_row * signed_row + signed_col * signed_col
        keep = (freq_row != rows_total // 2) & (freq_col != cols_total // 2)
        inverse = jnp.where(keep & (radius > 0.0), 1.0 / jnp.maximum(radius, 1.0), 0.0)
        n11 = signed_row * signed_row * inverse
        n12 = signed_row * signed_col * inverse
        n22 = signed_col * signed_col * inverse
        s_rr = held[at(c, 0), :]
        s_cc = held[at(c, 1), :]
        s_rc = held[at(c, 2), :]
        along_r = s_rr * n11 + s_rc * n12
        along_c = s_rc * n12 + s_cc * n22
        normal = BETA_REF * (along_r + along_c)
        cross = 0.5 * (n12 * (s_rr + s_cc) + s_rc * (n11 + n22))
        held[at(c, 0), :] = scale * (along_r * (1.0 / SHEAR_REF) - n11 * normal)
        held[at(c, 1), :] = scale * (along_c * (1.0 / SHEAR_REF) - n22 * normal)
        held[at(c, 2), :] = scale * (cross * (1.0 / SHEAR_REF) - n12 * normal)
    held[...] = dot3(split3(held[...]), wave, ((1,), (1,)))
    for n in range(3):
        v = []
        for c in range(RADIX):
            x = held[at(c, n), :span]
            y = held[at(c, n), span:]
            if c:
                cosine, sine = turn(c)
                x, y = x * cosine - y * sine, y * cosine + x * sine
            v.append((x, y))
        r02, r13 = v[0][0] + v[2][0], v[1][0] + v[3][0]
        d02, d13 = v[0][0] - v[2][0], v[1][0] - v[3][0]
        m02, m13 = v[0][1] + v[2][1], v[1][1] + v[3][1]
        e02, e13 = v[0][1] - v[2][1], v[1][1] - v[3][1]
        real = jnp.concatenate([r02 + r13, d02 - e13, r02 - r13, d02 + e13], axis=1)
        imag = jnp.concatenate([m02 + m13, e02 + d13, m02 - m13, e02 - d13], axis=1)
        for s in range(parts):
            out[s, 0, n] = real[:, s * rows : (s + 1) * rows]
            out[s, 1, n] = imag[:, s * rows : (s + 1) * rows]


def row_wave(span):
    ids = np.arange(span)
    angle = (np.outer(ids, ids) % span) * (2.0 * math.pi / span)
    cosine, sine = np.cos(angle), np.sin(angle)
    full = np.block([[cosine, -sine], [sine, cosine]]).astype(np.float32)
    high = full.astype(jnp.bfloat16)
    low = (full - high.astype(np.float32)).astype(jnp.bfloat16)
    turns = []
    for c in range(RADIX):
        angle = ids * c * (2.0 * math.pi / (RADIX * span))
        turns += [np.cos(angle), np.sin(angle)]
    return np.stack(turns).astype(np.float32), high, low


def run_rows(places, recv, tables, rows_total, cols_total, after):
    parts, _, _, part, rows = recv.shape
    dense = rows % 128 == 0
    if not dense:
        recv = jnp.transpose(recv, (1, 2, 3, 0, 4)).reshape(1, 2, 3, part, rows_total)
    span = rows_total // RADIX

    def kernel(*refs):
        rows_kernel(rows_total, cols_total, *refs)

    whole = pl.BlockSpec(memory_space=pltpu.VMEM)
    out = pl.pallas_call(
        kernel,
        in_specs=[pl.BlockSpec(memory_space=pltpu.SMEM), whole, whole, whole, whole, *any_specs(after)],
        out_specs=whole,
        out_shape=jax.ShapeDtypeStruct(recv.shape, jnp.float32),
        scratch_shapes=[pltpu.VMEM((RADIX * 3 * part, 2 * span), jnp.float32)],
        compiler_params=pltpu.CompilerParams(vmem_limit_bytes=VMEM_LIMIT),
        name="row_lines",
    )(places, recv, *tables, *after)
    if not dense:
        out = jnp.transpose(out.reshape(2, 3, part, parts, rows), (3, 0, 1, 2, 4))
    return out


def column_waves(freqs, ids, length):
    product = freqs[:, None] * ids[None, :] % length
    angle = product.astype(jnp.float32) * (2.0 * math.pi / length)
    full = jnp.concatenate([jnp.cos(angle), -jnp.sin(angle)], axis=0)[None]
    rounded = lax.reduce_precision(full, 8, 7)
    return rounded.astype(jnp.bfloat16), (full - rounded).astype(jnp.bfloat16)


def body(
    order_field,
    grain_label,
    phase_label,
    grain_mobility,
    stiff_index,
    stiff_table,
    eigen_strain,
    macro_strain,
):
    layers, _, rows, cols = order_field.shape
    parts = lax.axis_size("row")
    if lax.axis_size("grp") != 2 or layers != 2 or lax.axis_size("col") != 2:
        raise ValueError("unsupported split")
    group = lax.axis_index("grp").astype(jnp.int32)
    row_place = lax.axis_index("row").astype(jnp.int32)
    col_place = lax.axis_index("col").astype(jnp.int32)
    rows_total = rows * parts
    cols_total = cols * 2
    inner = group
    outer = 1 - group
    swap_pairs = [(0, 1), (1, 0)]
    ring_up = [(i, (i + 1) % parts) for i in range(parts)]
    ring_down = [(j, i) for i, j in ring_up]

    def swap_cols(value):
        return lax.ppermute(value, "col", swap_pairs)

    def swap_layers(value):
        return lax.ppermute(value, "grp", swap_pairs)

    remote_field = swap_layers(lax.dynamic_slice_in_dim(order_field, outer, 1, 0))

    mobility, stiff, top, bottom, sides = run_prepare(
        order_field, grain_label, phase_label, grain_mobility, stiff_index, stiff_table
    )

    def move_edges(top, bottom, sides):
        return (
            lax.ppermute(bottom, "row", ring_up),
            lax.ppermute(top, "row", ring_down),
            swap_cols(sides),
        )

    edges = move_edges(top, bottom, sides)
    stiff_far = swap_cols(stiff)
    signs = (1 - 2 * col_place).astype(jnp.float32)[None]
    strain_table = eigen_strain.reshape(-1)
    waves = column_waves(
        2 * jnp.arange(cols_total // 4, dtype=jnp.int32) + col_place,
        jnp.arange(cols, dtype=jnp.int32),
        cols_total,
    )
    tables = row_wave(rows_total // RADIX)

    def places(phi_at, other_at, layer):
        zero = jnp.zeros((), jnp.int32)
        return jnp.stack([zero + phi_at, zero + other_at, layer, row_place, col_place])

    def exchange(value):
        return lax.all_to_all(value, "row", split_axis=0, concat_axis=0, tiled=True)

    def stencil(fields, phi_at, other, other_at, remote, layer, own_edges, emit, after=()):
        return run_stencil(
            places(phi_at, other_at, layer),
            fields,
            other,
            remote,
            mobility,
            own_edges,
            edges,
            strain_table,
            emit,
            after,
        )

    here = {"inner": places(0, 0, inner), "outer": places(0, 0, outer)}

    def forward(name, eigen, eigen_far, swap, after=()):
        return run_forward(
            here[name],
            signs,
            macro_strain,
            stiff,
            stiff_far,
            eigen,
            eigen_far,
            swap,
            waves,
            parts,
            after,
        )

    def lines(name, recv, after=()):
        return run_rows(here[name], recv, tables, rows_total, cols_total, after)

    def columns(recv, after=()):
        mine = run_inverse(recv, waves, after)
        return mine, swap_cols(mine)

    def drive(name, pre, fields, eigen, swaps, held):
        return run_drive(
            here[name],
            pre,
            fields,
            mobility,
            stiff,
            eigen,
            strain_table,
            signs,
            macro_strain,
            swaps,
            held,
        )

    middle_inner, eigen_inner, *rim_inner = stencil(
        order_field, inner, order_field, outer, None, inner, edges, True, waves
    )
    far_inner = swap_cols(eigen_inner)
    sent = exchange(forward("inner", eigen_inner, far_inner, None))
    partial = stencil(order_field, outer, order_field, inner, None, outer, edges, False)
    edges_inner = move_edges(*rim_inner)
    back = exchange(lines("inner", sent, (partial,)))
    swaps_inner = [columns(back)]
    held_back = forward("inner", eigen_inner, far_inner, swaps_inner[0])
    sent_inner = exchange(held_back)

    middle_outer, eigen_outer, *rim_outer = run_finish(
        here["outer"], partial, remote_field, mobility, strain_table, (held_back,)
    )
    far_outer = swap_cols(eigen_outer)
    first_outer = forward("outer", eigen_outer, far_outer, None)
    sent_outer = exchange(first_outer)
    remote_middle = swap_layers(middle_outer)
    edges_outer = move_edges(*rim_outer)
    spread_inner = lines("inner", sent_inner)
    back_inner = exchange(spread_inner)
    pre_inner = stencil(middle_inner, 0, middle_outer, 0, None, inner, edges_inner, False)
    spread_outer = lines("outer", sent_outer, (pre_inner,))
    back_outer = exchange(spread_outer)
    swaps_inner.append(columns(back_inner))
    swaps_outer = [columns(back_outer)]
    sent_outer = exchange(forward("outer", eigen_outer, far_outer, swaps_outer[0]))
    held = drive("inner", pre_inner, middle_inner, eigen_inner, swaps_inner, None)
    back_outer = exchange(lines("outer", sent_outer, held))
    pre_outer = stencil(
        middle_outer, 0, middle_inner, 0, remote_middle, outer, edges_outer, False
    )
    swaps_outer.append(columns(back_outer, (pre_outer,)))
    return drive("outer", pre_outer, middle_outer, eigen_outer, swaps_outer, held)


def solution(mesh):
    return jax.shard_map(
        body,
        mesh=mesh,
        in_specs=(
            P("grp", None, "row", "col"),
            P("grp", "row", "col"),
            P("grp", "row", "col"),
            P(),
            P(),
            P(),
            P(),
            P(),
        ),
        out_specs=(P("grp", None, "row", "col"), P("grp", None, "row", "col")),
        check_vma=False,
    )
```

```python
import math

import jax
import jax.numpy as jnp
import numpy as np
from jax import lax
from jax.experimental import pallas as pl
from jax.experimental.pallas import tpu as pltpu
from jax.sharding import PartitionSpec as P


ITERS = 2
GAMMA_MIX = 1.5
KAPPA_GRAD = 1.0
STEP_TIME = 0.1
LAYER_COUPLE = 0.5
LAMBDA_REF = 1.25
SHEAR_REF = 1.25
BETA_REF = (LAMBDA_REF + SHEAR_REF) / (SHEAR_REF * (LAMBDA_REF + 2.0 * SHEAR_REF))
STRIP = 8
LANES = 128
RADIX = 4
VMEM_LIMIT = 56 * 1024 * 1024
VMEM_SMALL = 16 * 1024 * 1024


def split3(value):
    high = value.astype(jnp.bfloat16)
    low = (value - high.astype(jnp.float32)).astype(jnp.bfloat16)
    return high, low


def dot3(left, right, dims):
    left_high, left_low = left
    right_high, right_low = right

    def product(a, b):
        return lax.dot_general(a, b, (dims, ((), ())), preferred_element_type=jnp.float32)

    return product(left_high, right_high) + (
        product(left_high, right_low) + product(left_low, right_high)
    )


def shift_rows(value, before, after):
    place = lax.broadcasted_iota(jnp.int32, value.shape, 0)
    size = value.shape[0]
    upper = jnp.where(place == 0, before, pltpu.roll(value, 1, 0))
    lower = jnp.where(place == size - 1, after, pltpu.roll(value, size - 1, 0))
    return upper, lower


def shift_cols(value, before, after):
    size = value.shape[1]
    lanes = min(size, LANES)
    place = lax.broadcasted_iota(jnp.int32, (value.shape[0], lanes), 1)
    left = pltpu.roll(value, 1, 1)
    right = pltpu.roll(value, size - 1, 1)
    head = jnp.where(place == 0, before, left[:, :lanes])
    tail = jnp.where(place == lanes - 1, after, right[:, size - lanes :])
    if size == lanes:
        return head, tail
    return (
        jnp.concatenate([head, left[:, lanes:]], axis=1),
        jnp.concatenate([right[:, : size - lanes], tail], axis=1),
    )


def put_lane(packed, lane, column):
    place = lax.broadcasted_iota(jnp.int32, packed.shape, 1)
    return jnp.where(place == lane, column, packed)


def prepare_kernel(
    which, grain, phase, top_rows, bottom_rows, left, right, whole, speeds, index, table,
    mobility, stiff, edge_up, edge_dn, edge_col, layer,
):
    layer[...] = whole[...]
    count, rows = left.shape[1], left.shape[2]
    width = left.shape[3]
    labels = grain[0]
    speed = jnp.zeros(labels.shape, jnp.float32)
    for entry in range(speeds.shape[0]):
        speed = jnp.where(labels == entry, speeds[entry], speed)
    mobility[0] = speed
    labels = phase[0]
    lam = jnp.zeros(labels.shape, jnp.float32)
    shear = jnp.zeros(labels.shape, jnp.float32)
    for entry in range(index.shape[0]):
        match = labels == entry
        lam = jnp.where(match, table[index[entry], 0], lam)
        shear = jnp.where(match, table[index[entry], 1], shear)
    stiff[0, 0] = lam
    stiff[0, 1] = shear
    packed = jnp.zeros((rows, LANES), jnp.float32)
    for i in range(count):
        packed = put_lane(packed, i, left[0, i, :, 0:1])
        packed = put_lane(packed, count + 1 + i, right[0, i, :, width - 1 : width])
    packed = put_lane(packed, count, speed[:, 0:1])
    packed = put_lane(packed, 2 * count + 1, speed[:, speed.shape[1] - 1 :])
    edge_col[0] = packed[:, : 2 * count + 2]
    block = pl.program_id(1)

    @pl.when(block == 0)
    def _():
        for i in range(count):
            edge_up[0, i : i + 1, :] = top_rows[0, i, 0:1, :]
            edge_dn[0, i : i + 1, :] = bottom_rows[0, i, STRIP - 1 : STRIP, :]
        edge_up[0, count : count + 1, :] = speed[0:1, :]

    @pl.when(block == pl.num_programs(1) - 1)
    def _():
        edge_dn[0, count : count + 1, :] = speed[rows - 1 : rows, :]


def run_prepare(
    order_field, grain_label, phase_label, grain_mobility, stiff_index, stiff_table, which
):
    layers, count, rows, cols = order_field.shape
    block = min(rows, 8 * STRIP)
    width = min(cols, LANES)
    steps = rows // block
    piece = rows // (layers * steps)
    smem = pl.BlockSpec(memory_space=pltpu.SMEM)
    shape = jax.ShapeDtypeStruct
    return pl.pallas_call(
        prepare_kernel,
        grid_spec=pltpu.PrefetchScalarGridSpec(
        num_scalar_prefetch=1,
        grid=(layers, steps),
        in_specs=[
            pl.BlockSpec((1, block, cols), lambda l, r, w: (l, r, 0)),
            pl.BlockSpec((1, block, cols), lambda l, r, w: (l, r, 0)),
            pl.BlockSpec((1, count, STRIP, cols), lambda l, r, w: (l, 0, 0, 0)),
            pl.BlockSpec((1, count, STRIP, cols), lambda l, r, w: (l, 0, rows // STRIP - 1, 0)),
            pl.BlockSpec((1, count, block, width), lambda l, r, w: (l, 0, r, 0)),
            pl.BlockSpec((1, count, block, width), lambda l, r, w: (l, 0, r, cols // width - 1)),
            pl.BlockSpec((1, count, piece, cols), lambda l, r, w: (w[0], 0, l * steps + r, 0)),
            smem,
            smem,
            smem,
        ],
        out_specs=(
            pl.BlockSpec((1, block, cols), lambda l, r, w: (l, r, 0)),
            pl.BlockSpec((1, 2, block, cols), lambda l, r, w: (l, 0, r, 0)),
            pl.BlockSpec((1, count + 1, cols), lambda l, r, w: (l, 0, 0)),
            pl.BlockSpec((1, count + 1, cols), lambda l, r, w: (l, 0, 0)),
            pl.BlockSpec((1, block, 2 * count + 2), lambda l, r, w: (l, r, 0)),
            pl.BlockSpec((1, count, piece, cols), lambda l, r, w: (0, 0, l * steps + r, 0)),
        ),
        ),
        out_shape=(
            shape((layers, rows, cols), jnp.float32),
            shape((layers, 2, rows, cols), jnp.float32),
            shape((layers, count + 1, cols), jnp.float32),
            shape((layers, count + 1, cols), jnp.float32),
            shape((layers, rows, 2 * count + 2), jnp.float32),
            shape((1, count, rows, cols), jnp.float32),
        ),
        compiler_params=pltpu.CompilerParams(vmem_limit_bytes=VMEM_LIMIT),
        name="prepare",
    )(
        which, grain_label, phase_label, order_field, order_field, order_field, order_field,
        order_field, grain_mobility, stiff_index, stiff_table,
    )


def pack_sides(fields, out_col):
    count, rows, cols = fields.shape[1:]
    packed = jnp.zeros((rows, LANES), jnp.float32)
    for i in range(count):
        packed = put_lane(packed, i, fields[0, i, :, 0:1])
        packed = put_lane(packed, count + i, fields[0, i, :, cols - 1 : cols])
    out_col[0] = packed[:, : 2 * count]


def emit_rim(fields, out_up, out_dn, out_col):
    count, rows, _ = fields.shape[1:]
    pack_sides(fields, out_col)

    @pl.when(pl.program_id(0) == 0)
    def _():
        for i in range(count):
            out_up[0, i : i + 1, :] = fields[0, i, 0:1, :]

    @pl.when(pl.program_id(0) == pl.num_programs(0) - 1)
    def _():
        for i in range(count):
            out_dn[0, i : i + 1, :] = fields[0, i, rows - 1 : rows, :]


def stencil_kernel(has_remote, emit, waits, count, *refs):
    refs = list(refs)
    refs.pop(0)
    phi, phi_up, phi_dn, other = (refs.pop(0) for _ in range(4))
    remote = refs.pop(0) if has_remote else None
    mob, mob_up, mob_dn = (refs.pop(0) for _ in range(3))
    edge_up, edge_dn, edge_col = (refs.pop(0) for _ in range(3))
    mob_edge_up, mob_edge_dn, mob_edge_col = (refs.pop(0) for _ in range(3))
    eigen_strain = refs.pop(0)
    del refs[:waits]
    out = refs.pop(0)
    if emit:
        out_eigen, out_up, out_dn, out_col = refs
    block = pl.program_id(0)
    first = block == 0
    last = block == pl.num_programs(0) - 1
    rows, _ = phi.shape[2:]
    strips = rows // STRIP
    side = edge_col.shape[2] // 2
    mob_side = mob_edge_col.shape[2] // 2

    def strip_body(strip, carry):
        start = pl.multiple_of(strip * STRIP, STRIP)
        here = pl.ds(start, STRIP)
        at_top = strip == 0
        at_bottom = strip == strips - 1

        def before_after(main, up, dn, edge_before, edge_after):
            before = jnp.where(
                at_top,
                jnp.where(first, edge_before, up),
                main(pl.ds(jnp.maximum(start - 1, 0), 1)),
            )
            after = jnp.where(
                at_bottom,
                jnp.where(last, edge_after, dn),
                main(pl.ds(jnp.minimum(start + STRIP, rows - 1), 1)),
            )
            return before, after

        m = mob[0, here, :]
        before, after = before_after(
            lambda r: mob[0, r, :],
            mob_up[0, STRIP - 1 : STRIP, :],
            mob_dn[0, 0:1, :],
            mob_edge_up[0, count : count + 1, :],
            mob_edge_dn[0, count : count + 1, :],
        )
        m_up, m_dn = shift_rows(m, before, after)
        m_edges = mob_edge_col[0, here, :]
        m_left, m_right = shift_cols(
            m,
            m_edges[:, mob_side + count : mob_side + count + 1],
            m_edges[:, count : count + 1],
        )
        half_step = 0.5 * STEP_TIME * KAPPA_GRAD
        w_up = half_step * (m + m_up)
        w_dn = half_step * (m + m_dn)
        w_left = half_step * (m + m_left)
        w_right = half_step * (m + m_right)
        total = jnp.zeros_like(m)
        for i in range(count):
            value = phi[0, i, here, :]
            total = total + value * value
        scaled = STEP_TIME * m
        base = (
            1.0
            - (w_up + w_dn + w_left + w_right)
            + scaled * ((1.0 - 2.0 * LAYER_COUPLE) - 2.0 * GAMMA_MIX * total)
        )
        coupling = LAYER_COUPLE * scaled
        cubic = (2.0 * GAMMA_MIX - 1.0) * scaled
        if emit:
            sums = [jnp.zeros_like(m) for _ in range(3)]
        edges = edge_col[0, here, :]
        for i in range(count):
            value = phi[0, i, here, :]
            before, after = before_after(
                lambda r: phi[0, i, r, :],
                phi_up[0, i, STRIP - 1 : STRIP, :],
                phi_dn[0, i, 0:1, :],
                edge_up[0, i : i + 1, :],
                edge_dn[0, i : i + 1, :],
            )
            upper, lower = shift_rows(value, before, after)
            left, right = shift_cols(
                value, edges[:, side + i : side + i + 1], edges[:, i : i + 1]
            )
            beside = other[0, i, here, :]
            if has_remote:
                beside = beside + remote[0, i, here, :]
            result = (
                value * (base + cubic * (value * value))
                + coupling * beside
                + (w_up * upper + w_dn * lower)
                + (w_left * left + w_right * right)
            )
            out[0, i, here, :] = result
            if emit:
                square = result * result
                for c in range(3):
                    sums[c] = sums[c] + square * eigen_strain[3 * i + c]
        if emit:
            for c in range(3):
                out_eigen[c, here, :] = sums[c]
        return carry

    lax.fori_loop(0, strips, strip_body, 0)
    if emit:
        emit_rim(out, out_up, out_dn, out_col)


def rim_outputs(count, rows, cols, block):
    shape = jax.ShapeDtypeStruct
    shapes = (
        shape((1, count, rows, cols), jnp.float32),
        shape((3, rows, cols), jnp.float32),
        shape((1, count, cols), jnp.float32),
        shape((1, count, cols), jnp.float32),
        shape((1, rows, 2 * count), jnp.float32),
    )
    specs = (
        pl.BlockSpec((1, count, block, cols), lambda r, p: (0, 0, r, 0)),
        pl.BlockSpec((3, block, cols), lambda r, p: (0, r, 0)),
        pl.BlockSpec((1, count, cols), lambda r, p: (0, 0, 0)),
        pl.BlockSpec((1, count, cols), lambda r, p: (0, 0, 0)),
        pl.BlockSpec((1, block, 2 * count), lambda r, p: (0, r, 0)),
    )
    return shapes, specs


def any_specs(values):
    return [pl.BlockSpec(memory_space=pl.ANY) for _ in values]


def run_stencil(
    places, fields, other, remote, mobility, edges, mob_edges, eigen_strain, emit, after=()
):
    _, rows, cols = mobility.shape
    count = fields.shape[1]
    block = min(rows, 4 * STRIP)
    per = block // STRIP
    tops = rows // STRIP - 1
    has_remote = remote is not None
    spec = pl.BlockSpec

    def above(r):
        return jnp.maximum(r * per - 1, 0)

    def below(r):
        return jnp.minimum((r + 1) * per, tops)

    args = [fields, fields, fields, other]
    specs = [
        spec((1, count, block, cols), lambda r, p: (p[0], 0, r, 0)),
        spec((1, count, STRIP, cols), lambda r, p: (p[0], 0, above(r), 0)),
        spec((1, count, STRIP, cols), lambda r, p: (p[0], 0, below(r), 0)),
        spec((1, count, block, cols), lambda r, p: (p[1], 0, r, 0)),
    ]
    if has_remote:
        args.append(remote)
        specs.append(spec((1, count, block, cols), lambda r, p: (0, 0, r, 0)))
    args += [mobility, mobility, mobility]
    specs += [
        spec((1, block, cols), lambda r, p: (p[2], r, 0)),
        spec((1, STRIP, cols), lambda r, p: (p[2], above(r), 0)),
        spec((1, STRIP, cols), lambda r, p: (p[2], below(r), 0)),
    ]
    for group, at in ((edges, 0), (mob_edges, 2)):
        for rows_edge in group[:2]:
            args.append(rows_edge)
            specs.append(
                spec((1, rows_edge.shape[1], cols), lambda r, p, at=at: (p[at], 0, 0))
            )
        args.append(group[2])
        specs.append(
            spec((1, block, group[2].shape[2]), lambda r, p, at=at: (p[at], r, 0))
        )
    args += [eigen_strain, *after]
    specs += [spec(memory_space=pltpu.SMEM), *any_specs(after)]
    out_shape, out_specs = rim_outputs(count, rows, cols, block)
    if not emit:
        out_shape, out_specs = out_shape[0], out_specs[0]

    def kernel(*refs):
        stencil_kernel(has_remote, emit, len(after), count, *refs)

    return pl.pallas_call(
        kernel,
        grid_spec=pltpu.PrefetchScalarGridSpec(
            num_scalar_prefetch=1,
            grid=(rows // block,),
            in_specs=specs,
            out_specs=out_specs,
        ),
        out_shape=out_shape,
        compiler_params=pltpu.CompilerParams(vmem_limit_bytes=VMEM_LIMIT),
        name="stencil",
    )(places, *args)


def finish_kernel(waits, places, partial, remote, mob, eigen_strain, *refs):
    out, out_eigen, out_up, out_dn, out_col = refs[waits:]
    count, rows = out.shape[1:3]
    for start in range(0, rows, STRIP):
        here = slice(start, start + STRIP)
        coupling = (LAYER_COUPLE * STEP_TIME) * mob[0, here, :]
        sums = [jnp.zeros_like(coupling) for _ in range(3)]
        for i in range(count):
            result = partial[0, i, here, :] + coupling * remote[0, i, here, :]
            out[0, i, here, :] = result
            square = result * result
            for c in range(3):
                sums[c] = sums[c] + square * eigen_strain[3 * i + c]
        for c in range(3):
            out_eigen[c, here, :] = sums[c]
    emit_rim(out, out_up, out_dn, out_col)


def run_finish(places, partial, remote, mobility, eigen_strain, after):
    _, rows, cols = mobility.shape
    count = partial.shape[1]
    block = min(rows, 2 * STRIP)
    field = pl.BlockSpec((1, count, block, cols), lambda r, p: (0, 0, r, 0))
    out_shape, out_specs = rim_outputs(count, rows, cols, block)

    def kernel(*refs):
        finish_kernel(len(after), *refs)

    return pl.pallas_call(
        kernel,
        grid_spec=pltpu.PrefetchScalarGridSpec(
            num_scalar_prefetch=1,
            grid=(rows // block,),
            in_specs=[
                field,
                field,
                pl.BlockSpec((1, block, cols), lambda r, p: (p[2], r, 0)),
                pl.BlockSpec(memory_space=pltpu.SMEM),
                *any_specs(after),
            ],
            out_specs=out_specs,
        ),
        out_shape=out_shape,
        compiler_params=pltpu.CompilerParams(vmem_limit_bytes=VMEM_LIMIT),
        name="finish",
    )(places, partial, remote, mobility, eigen_strain, *after)


def drive_kernel(places, pre, phi, mob, stiff, eigen, eigen_strain, signs, macro, *refs):
    swaps = [(refs[2 * k], refs[2 * k + 1]) for k in range(ITERS)]
    out, out_strain = refs[-2:]
    count, rows = phi.shape[1:3]
    sign = signs[0]
    for start in range(0, rows, STRIP):
        here = slice(start, start + STRIP)
        lam = stiff[0, 0, here, :]
        shear2 = 2.0 * stiff[0, 1, here, :]
        elastic = []
        for c in range(3):
            strain = macro[c]
            for mine, theirs in swaps:
                strain = strain - (theirs[c, here, :] + sign * mine[c, here, :])
            out_strain[0, c, here, :] = strain
            elastic.append(strain - eigen[c, here, :])
        spread = lam * (elastic[0] + elastic[1])
        push = (2.0 * STEP_TIME) * mob[0, here, :]
        sigma = (
            push * (spread + shear2 * elastic[0]),
            push * (spread + shear2 * elastic[1]),
            push * (2.0 * shear2 * elastic[2]),
        )
        for i in range(count):
            force = (
                sigma[0] * eigen_strain[3 * i]
                + sigma[1] * eigen_strain[3 * i + 1]
                + sigma[2] * eigen_strain[3 * i + 2]
            )
            out[0, i, here, :] = pre[0, i, here, :] + phi[0, i, here, :] * force


def run_drive(places, pre, fields, mobility, stiff, eigen, eigen_strain, signs, macro, swaps, held):
    layers, rows, cols = mobility.shape
    count = fields.shape[1]
    block = min(rows, 2 * STRIP)
    smem = pl.BlockSpec(memory_space=pltpu.SMEM)
    field = pl.BlockSpec((1, count, block, cols), lambda r, p: (0, 0, r, 0))
    plane = pl.BlockSpec((3, block, cols), lambda r, p: (0, r, 0))
    args = [pre, fields, mobility, stiff, eigen, eigen_strain, signs, macro]
    specs = [
        field,
        field,
        pl.BlockSpec((1, block, cols), lambda r, p: (p[2], r, 0)),
        pl.BlockSpec((1, 2, block, cols), lambda r, p: (p[2], 0, r, 0)),
        plane,
        smem,
        smem,
        smem,
    ]
    for pair in swaps:
        args += list(pair)
        specs += [plane, plane]
    aliases = {}
    if held is not None:
        aliases = {1 + len(args): 0, 2 + len(args): 1}
        args += list(held)
        specs += any_specs(held)
    return pl.pallas_call(
        drive_kernel,
        grid_spec=pltpu.PrefetchScalarGridSpec(
            num_scalar_prefetch=1,
            grid=(rows // block,),
            in_specs=specs,
            out_specs=(
                pl.BlockSpec((1, count, block, cols), lambda r, p: (p[2], 0, r, 0)),
                pl.BlockSpec((1, 3, block, cols), lambda r, p: (p[2], 0, r, 0)),
            ),
        ),
        out_shape=(
            jax.ShapeDtypeStruct((layers, count, rows, cols), jnp.float32),
            jax.ShapeDtypeStruct((layers, 3, rows, cols), jnp.float32),
        ),
        input_output_aliases=aliases,
        compiler_params=pltpu.CompilerParams(vmem_limit_bytes=VMEM_LIMIT),
        name="drive",
    )(places, *args)


def forward_kernel(has_swap, parts, waits, *refs):
    refs = list(refs)
    refs.pop(0)
    signs, macro, stiff, stiff_far, eigen, eigen_far = (refs.pop(0) for _ in range(6))
    swap = (refs.pop(0), refs.pop(0)) if has_swap else None
    high, low = refs.pop(0), refs.pop(0)
    out, flat = refs[waits:]
    rows = eigen.shape[1]
    sign = signs[0]
    near = []
    far = []
    for c in range(3):
        strain = strain_far = macro[c]
        if has_swap:
            mine = swap[0][c]
            theirs = swap[1][c]
            strain = strain - (theirs + sign * mine)
            strain_far = strain_far - (mine - sign * theirs)
        near.append(strain - eigen[c])
        far.append(strain_far - eigen_far[c])

    def stress(elastic, table):
        lam = table[0, 0]
        shear2 = 2.0 * table[0, 1]
        spread = lam * (elastic[0] + elastic[1])
        return (
            spread + shear2 * elastic[0],
            spread + shear2 * elastic[1],
            shear2 * elastic[2],
        )

    near = stress(near, stiff)
    far = stress(far, stiff_far)
    for c in range(3):
        flat[c * rows : (c + 1) * rows, :] = far[c] + sign * near[c]
    result = dot3((high[0], low[0]), split3(flat[...]), ((1,), (1,)))
    width = result.shape[0] // 2
    part = width // parts
    for q in range(parts):
        for side in range(2):
            at = side * width + q * part
            for c in range(3):
                out[q, side, c] = result[at : at + part, c * rows : (c + 1) * rows]


def run_forward(places, signs, macro, stiff, stiff_far, eigen, eigen_far, swap, waves, parts, after):
    rows, cols = eigen.shape[1:]
    width = waves[0].shape[1]
    smem = pl.BlockSpec(memory_space=pltpu.SMEM)
    plane = pl.BlockSpec((3, rows, cols), lambda g, p: (0, 0, 0))
    table = pl.BlockSpec((1, 2, rows, cols), lambda g, p: (p[2], 0, 0, 0))
    wave = pl.BlockSpec((1, width, cols), lambda g, p: (0, 0, 0))
    args = [signs, macro, stiff, stiff_far, eigen, eigen_far]
    specs = [smem, smem, table, table, plane, plane]
    if swap is not None:
        args += list(swap)
        specs += [plane, plane]
    args += list(waves)
    specs += [wave, wave]
    args += list(after)
    specs += any_specs(after)
    shape = (parts, 2, 3, width // (2 * parts), rows)

    def kernel(*refs):
        forward_kernel(swap is not None, parts, len(after), *refs)

    return pl.pallas_call(
        kernel,
        grid_spec=pltpu.PrefetchScalarGridSpec(
            num_scalar_prefetch=1,
            grid=(1,),
            in_specs=specs,
            out_specs=pl.BlockSpec(shape, lambda g, p: (0, 0, 0, 0, 0)),
            scratch_shapes=[pltpu.VMEM((3 * rows, cols), jnp.float32)],
        ),
        out_shape=jax.ShapeDtypeStruct(shape, jnp.float32),
        compiler_params=pltpu.CompilerParams(vmem_limit_bytes=VMEM_LIMIT),
        name="forward_columns",
    )(places, *args)


def inverse_kernel(recv, high, low, *refs):
    out, flat = refs[-2:]
    parts, _, _, part, rows = recv.shape
    width = parts * part
    for q in range(parts):
        for side in range(2):
            at = side * width + q * part
            for c in range(3):
                flat[at : at + part, c * rows : (c + 1) * rows] = recv[q, side, c]
    result = dot3(split3(flat[...]), (high[0], low[0]), ((0,), (0,)))
    for c in range(3):
        out[c] = result[c * rows : (c + 1) * rows, :]


def run_inverse(recv, waves, after):
    _, _, _, _, rows = recv.shape
    _, width, cols = waves[0].shape
    whole = pl.BlockSpec(memory_space=pltpu.VMEM)
    return pl.pallas_call(
        inverse_kernel,
        in_specs=[whole, whole, whole, *any_specs(after)],
        out_specs=whole,
        out_shape=jax.ShapeDtypeStruct((3, rows, cols), jnp.float32),
        scratch_shapes=[pltpu.VMEM((width, 3 * rows), jnp.float32)],
        compiler_params=pltpu.CompilerParams(vmem_limit_bytes=VMEM_SMALL),
        name="inverse_columns",
    )(recv, *waves, *after)


def rows_kernel(rows_total, cols_total, places, recv, turns, high, low, *refs):
    out, held = refs[-2:]
    parts, _, _, part, rows = recv.shape
    span = rows_total // RADIX

    def turn(c):
        return turns[2 * c : 2 * c + 1, :], turns[2 * c + 1 : 2 * c + 2, :]

    def at(c, n):
        start = (c * 3 + n) * part
        return slice(start, start + part)

    def gather(side, n):
        if parts == 1:
            return recv[0, side, n]
        return jnp.concatenate([recv[s, side, n] for s in range(parts)], axis=1)

    for n in range(3):
        real = gather(0, n)
        imag = gather(1, n)
        r = [real[:, a * span : (a + 1) * span] for a in range(RADIX)]
        m = [imag[:, a * span : (a + 1) * span] for a in range(RADIX)]
        r02, r13, d02, d13 = r[0] + r[2], r[1] + r[3], r[0] - r[2], r[1] - r[3]
        m02, m13, e02, e13 = m[0] + m[2], m[1] + m[3], m[0] - m[2], m[1] - m[3]
        mixed = (
            (r02 + r13, m02 + m13),
            (d02 + e13, e02 - d13),
            (r02 - r13, m02 - m13),
            (d02 - e13, e02 + d13),
        )
        for c in range(RADIX):
            x, y = mixed[c]
            if c:
                cosine, sine = turn(c)
                x, y = x * cosine + y * sine, y * cosine - x * sine
            held[at(c, n), :span] = x
            held[at(c, n), span:] = y
    wave = (high[...], low[...])
    held[...] = dot3(split3(held[...]), wave, ((1,), (0,)))

    lanes = lax.broadcasted_iota(jnp.int32, (part, 2 * span), 1)
    lanes = jnp.where(lanes >= span, lanes - span, lanes)
    lines = lax.broadcasted_iota(jnp.int32, (part, 2 * span), 0)
    freq_col = 2 * (places[3] * part + lines) + places[4]
    signed_col = freq_col.astype(jnp.float32)
    scale = jnp.where(freq_col == 0, 1.0, 2.0) * (1.0 / (rows_total * cols_total))
    for c in range(RADIX):
        freq_row = RADIX * lanes + c
        signed_row = jnp.where(
            freq_row >= rows_total // 2, freq_row - rows_total, freq_row
        ).astype(jnp.float32)
        radius = signed_row * signed_row + signed_col * signed_col
        keep = (freq_row != rows_total // 2) & (freq_col != cols_total // 2)
        inverse = jnp.where(keep & (radius > 0.0), 1.0 / jnp.maximum(radius, 1.0), 0.0)
        n11 = signed_row * signed_row * inverse
        n12 = signed_row * signed_col * inverse
        n22 = signed_col * signed_col * inverse
        s_rr = held[at(c, 0), :]
        s_cc = held[at(c, 1), :]
        s_rc = held[at(c, 2), :]
        along_r = s_rr * n11 + s_rc * n12
        along_c = s_rc * n12 + s_cc * n22
        normal = BETA_REF * (along_r + along_c)
        cross = 0.5 * (n12 * (s_rr + s_cc) + s_rc * (n11 + n22))
        held[at(c, 0), :] = scale * (along_r * (1.0 / SHEAR_REF) - n11 * normal)
        held[at(c, 1), :] = scale * (along_c * (1.0 / SHEAR_REF) - n22 * normal)
        held[at(c, 2), :] = scale * (cross * (1.0 / SHEAR_REF) - n12 * normal)
    held[...] = dot3(split3(held[...]), wave, ((1,), (1,)))
    for n in range(3):
        v = []
        for c in range(RADIX):
            x = held[at(c, n), :span]
            y = held[at(c, n), span:]
            if c:
                cosine, sine = turn(c)
                x, y = x * cosine - y * sine, y * cosine + x * sine
            v.append((x, y))
        r02, r13 = v[0][0] + v[2][0], v[1][0] + v[3][0]
        d02, d13 = v[0][0] - v[2][0], v[1][0] - v[3][0]
        m02, m13 = v[0][1] + v[2][1], v[1][1] + v[3][1]
        e02, e13 = v[0][1] - v[2][1], v[1][1] - v[3][1]
        real = jnp.concatenate([r02 + r13, d02 - e13, r02 - r13, d02 + e13], axis=1)
        imag = jnp.concatenate([m02 + m13, e02 + d13, m02 - m13, e02 - d13], axis=1)
        for s in range(parts):
            out[s, 0, n] = real[:, s * rows : (s + 1) * rows]
            out[s, 1, n] = imag[:, s * rows : (s + 1) * rows]


def row_wave(span):
    ids = np.arange(span)
    angle = (np.outer(ids, ids) % span) * (2.0 * math.pi / span)
    cosine, sine = np.cos(angle), np.sin(angle)
    full = np.block([[cosine, -sine], [sine, cosine]]).astype(np.float32)
    high = full.astype(jnp.bfloat16)
    low = (full - high.astype(np.float32)).astype(jnp.bfloat16)
    turns = []
    for c in range(RADIX):
        angle = ids * c * (2.0 * math.pi / (RADIX * span))
        turns += [np.cos(angle), np.sin(angle)]
    return np.stack(turns).astype(np.float32), high, low


def run_rows(places, recv, tables, rows_total, cols_total, after):
    parts, _, _, part, rows = recv.shape
    dense = rows % 128 == 0
    if not dense:
        recv = jnp.transpose(recv, (1, 2, 3, 0, 4)).reshape(1, 2, 3, part, rows_total)
    span = rows_total // RADIX

    def kernel(*refs):
        rows_kernel(rows_total, cols_total, *refs)

    whole = pl.BlockSpec(memory_space=pltpu.VMEM)
    out = pl.pallas_call(
        kernel,
        in_specs=[pl.BlockSpec(memory_space=pltpu.SMEM), whole, whole, whole, whole, *any_specs(after)],
        out_specs=whole,
        out_shape=jax.ShapeDtypeStruct(recv.shape, jnp.float32),
        scratch_shapes=[pltpu.VMEM((RADIX * 3 * part, 2 * span), jnp.float32)],
        compiler_params=pltpu.CompilerParams(vmem_limit_bytes=VMEM_SMALL),
        name="row_lines",
    )(places, recv, *tables, *after)
    if not dense:
        out = jnp.transpose(out.reshape(2, 3, part, parts, rows), (3, 0, 1, 2, 4))
    return out


def column_waves(freqs, ids, length):
    product = freqs[:, None] * ids[None, :] % length
    angle = product.astype(jnp.float32) * (2.0 * math.pi / length)
    full = jnp.concatenate([jnp.cos(angle), -jnp.sin(angle)], axis=0)[None]
    rounded = lax.reduce_precision(full, 8, 7)
    return rounded.astype(jnp.bfloat16), (full - rounded).astype(jnp.bfloat16)


def body(
    order_field,
    grain_label,
    phase_label,
    grain_mobility,
    stiff_index,
    stiff_table,
    eigen_strain,
    macro_strain,
):
    layers, _, rows, cols = order_field.shape
    parts = lax.axis_size("row")
    if lax.axis_size("grp") != 2 or layers != 2 or lax.axis_size("col") != 2:
        raise ValueError("unsupported split")
    group = lax.axis_index("grp").astype(jnp.int32)
    row_place = lax.axis_index("row").astype(jnp.int32)
    col_place = lax.axis_index("col").astype(jnp.int32)
    rows_total = rows * parts
    cols_total = cols * 2
    inner = group
    outer = 1 - group
    swap_pairs = [(0, 1), (1, 0)]
    ring_up = [(i, (i + 1) % parts) for i in range(parts)]
    ring_down = [(j, i) for i, j in ring_up]

    def swap_cols(value):
        return lax.ppermute(value, "col", swap_pairs)

    def swap_layers(value):
        return lax.ppermute(value, "grp", swap_pairs)

    mobility, stiff, top, bottom, sides, edge_layer = run_prepare(
        order_field,
        grain_label,
        phase_label,
        grain_mobility,
        stiff_index,
        stiff_table,
        outer[None],
    )
    remote_field = swap_layers(edge_layer)

    def move_edges(top, bottom, sides):
        return (
            lax.ppermute(bottom, "row", ring_up),
            lax.ppermute(top, "row", ring_down),
            swap_cols(sides),
        )

    edges = move_edges(top, bottom, sides)
    stiff_far = swap_cols(stiff)
    signs = (1 - 2 * col_place).astype(jnp.float32)[None]
    strain_table = eigen_strain.reshape(-1)
    waves = column_waves(
        2 * jnp.arange(cols_total // 4, dtype=jnp.int32) + col_place,
        jnp.arange(cols, dtype=jnp.int32),
        cols_total,
    )
    tables = row_wave(rows_total // RADIX)

    def places(phi_at, other_at, layer):
        zero = jnp.zeros((), jnp.int32)
        return jnp.stack([zero + phi_at, zero + other_at, layer, row_place, col_place])

    def exchange(value):
        return lax.all_to_all(value, "row", split_axis=0, concat_axis=0, tiled=True)

    def stencil(fields, phi_at, other, other_at, remote, layer, own_edges, emit, after=()):
        return run_stencil(
            places(phi_at, other_at, layer),
            fields,
            other,
            remote,
            mobility,
            own_edges,
            edges,
            strain_table,
            emit,
            after,
        )

    here = {"inner": places(0, 0, inner), "outer": places(0, 0, outer)}

    def forward(name, eigen, eigen_far, swap, after=()):
        return run_forward(
            here[name],
            signs,
            macro_strain,
            stiff,
            stiff_far,
            eigen,
            eigen_far,
            swap,
            waves,
            parts,
            after,
        )

    def lines(name, recv, after=()):
        return run_rows(here[name], recv, tables, rows_total, cols_total, after)

    def columns(recv, after=()):
        mine = run_inverse(recv, waves, after)
        return mine, swap_cols(mine)

    def drive(name, pre, fields, eigen, swaps, held):
        return run_drive(
            here[name],
            pre,
            fields,
            mobility,
            stiff,
            eigen,
            strain_table,
            signs,
            macro_strain,
            swaps,
            held,
        )

    middle_inner, eigen_inner, *rim_inner = stencil(
        order_field, inner, order_field, outer, None, inner, edges, True, waves
    )
    far_inner = swap_cols(eigen_inner)
    sent = exchange(forward("inner", eigen_inner, far_inner, None))
    partial = stencil(order_field, outer, order_field, inner, None, outer, edges, False)
    edges_inner = move_edges(*rim_inner)
    back = exchange(lines("inner", sent, (partial,)))
    swaps_inner = [columns(back)]
    held_back = forward("inner", eigen_inner, far_inner, swaps_inner[0])
    sent_inner = exchange(held_back)

    middle_outer, eigen_outer, *rim_outer = run_finish(
        here["outer"], partial, remote_field, mobility, strain_table, (held_back,)
    )
    far_outer = swap_cols(eigen_outer)
    first_outer = forward("outer", eigen_outer, far_outer, None)
    sent_outer = exchange(first_outer)
    remote_middle = swap_layers(middle_outer)
    edges_outer = move_edges(*rim_outer)
    spread_inner = lines("inner", sent_inner)
    back_inner = exchange(spread_inner)
    pre_inner = stencil(middle_inner, 0, middle_outer, 0, None, inner, edges_inner, False)
    spread_outer = lines("outer", sent_outer, (pre_inner,))
    back_outer = exchange(spread_outer)
    swaps_inner.append(columns(back_inner))
    swaps_outer = [columns(back_outer)]
    sent_outer = exchange(forward("outer", eigen_outer, far_outer, swaps_outer[0]))
    held = drive("inner", pre_inner, middle_inner, eigen_inner, swaps_inner, None)
    back_outer = exchange(lines("outer", sent_outer, held))
    pre_outer = stencil(
        middle_outer, 0, middle_inner, 0, remote_middle, outer, edges_outer, False
    )
    swaps_outer.append(columns(back_outer, (pre_outer,)))
    return drive("outer", pre_outer, middle_outer, eigen_outer, swaps_outer, held)


def solution(mesh):
    return jax.shard_map(
        body,
        mesh=mesh,
        in_specs=(
            P("grp", None, "row", "col"),
            P("grp", "row", "col"),
            P("grp", "row", "col"),
            P(),
            P(),
            P(),
            P(),
            P(),
        ),
        out_specs=(P("grp", None, "row", "col"), P("grp", None, "row", "col")),
        check_vma=False,
    )
```
